256 devices in a mesh: seq: 32 (over z, x), chan: 8 (over y, core).
Axes of the slice: x: 4, y: 4, z: 8, core: 2. Of those that a mesh axis runs over, the one named last changes fastest.
Arguments:
- tokens: int32 [8192], P('seq'), may hold values from 0 to 255
- embed_table: bfloat16 [256, 2048], P(None, 'chan'), may hold values from -6 to 6
- short_conv: float32 [3, 2048], P(None, 'chan'), may hold values from -4 to 4
- query_branch: bfloat16 [8192, 2048], P('seq', 'chan'), may hold values from -6 to 6
- key_branch: bfloat16 [8192, 2048], P('seq', 'chan'), may hold values from -6 to 6
- decay_rate: float32 [2048], P('chan'), may hold values from 1.2207031e-05 to 0.1, as said below
- weight_first: float32 [33, 64], replicated, may hold values from -1 to 1
- weight_second: float32 [64, 64], replicated, may hold values from -0.75 to 0.75
- weight_third: float32 [64, 2048], P(None, 'chan'), may hold values from -0.75 to 0.75
- skip_gain: float32 [2048], P('chan'), may hold values from -4 to 4
- cotangent: bfloat16 [8192, 2048], P('seq', 'chan'), may hold values from -6 to 6
Outputs:
- operator_out: bfloat16 [8192, 2048], P('seq', 'chan')
- grad_query: bfloat16 [8192, 2048], P('seq', 'chan')
- grad_key: bfloat16 [8192, 2048], P('seq', 'chan')
- grad_embed: float32 [256, 2048], P('seq', 'chan')
- grad_short: float32 [3, 2048], P(None, 'chan')
- grad_skip: float32 [2048], P('chan')
- grad_first: float32 [33, 64], replicated
- grad_second: float32 [64, 64], replicated
- grad_third: float32 [64, 2048], P(None, 'chan')
The draws below stay inside these ranges and needn't reach their ends.
Inputs may be any that keep to these rules, and one draw needn't show every extreme that they name: `decay_rate`: each channel's decay rate is either slow, log-uniform from 0.1 / 8192 to 2 / 8192, or fast, log-uniform from 0.02 to 0.1, clipped to the stated range.
All inputs are finite; a program needn't handle non-finite values.
Results may differ from the reference program's by a relative error of at most 0.0014.
Values sent between devices are 32-bit elements; how exact they have to be, the bound alone decides.
No kernel may reach another device: no remote copies, remote signals or barrier semaphores. Data moves between devices by JAX's collectives and lax.ppermute only.
A program may use at most 64 MiB of HBM per device.

```python
import math
import jax
import jax.numpy as jnp
from jax import lax

D = 2048
VOCAB = 256
FH = 64
BANDS = 16
FEAT = 33
SEQLEN = 8192


def draw_decay_rate(key, part):
    pick_key = jax.random.fold_in(key, 11)
    slow_key = jax.random.fold_in(key, 12)
    fast_key = jax.random.fold_in(key, 13)
    slow_share = 0.5
    chosen = jax.random.uniform(pick_key, (D,), jnp.float32) < slow_share
    slow_rate = jnp.exp(jax.random.uniform(slow_key, (D,), jnp.float32, math.log(0.1), math.log(2.0))) / SEQLEN
    fast_rate = jnp.exp(jax.random.uniform(fast_key, (D,), jnp.float32, math.log(0.02), math.log(0.1)))
    return jnp.clip(jnp.where(chosen, slow_rate, fast_rate), 0.1 / SEQLEN, 0.1).astype(jnp.float32)


def with_ends(drawn, rng, smallest, largest):
    place = [jax.random.randint(jax.random.fold_in(rng, axis), (), 0, length) for axis, length in enumerate(drawn.shape)]
    longest = drawn.shape.index(max(drawn.shape))
    beside = place[:longest] + [(place[longest] + 1) % drawn.shape[longest]] + place[longest + 1:]
    return drawn.at[tuple(place)].set(smallest).at[tuple(beside)].set(largest)


def block_scale(rng, extent, cuts, least, largest):
    def one(dim, parts):
        heights = jax.random.uniform(jax.random.fold_in(jax.random.fold_in(rng, 6), dim), (parts,), jnp.float32, least / len(cuts), largest / len(cuts))
        return jnp.repeat(jnp.exp(heights), extent[dim] // parts).reshape((-1,) + (1,) * (len(extent) - dim - 1))

    loudness = one(*cuts[0])
    for cut in cuts[1:]:
        loudness = loudness * one(*cut)
    return loudness


def scatter_about(rng, shape, deviation, most, shards=(), kind=jnp.bfloat16):
    array = deviation * jax.random.normal(rng, shape, jnp.float32)
    if shards:
        array = array * block_scale(rng, shape, shards, -0.22, 0.18)
    return jnp.clip(array, -most, most).astype(kind)


def setup_inputs(seed: int = 0) -> dict:
    splits = jax.random.split(jax.random.key(seed), 12)
    tokens = with_ends(jax.random.randint(splits[0], (SEQLEN,), 0, VOCAB), jax.random.fold_in(splits[0], 1), 0, VOCAB - 1).astype(jnp.int32)
    embed_table = scatter_about(splits[1], (VOCAB, D), 1.0, 6.0, ((1, 8),))
    short_conv = scatter_about(splits[2], (3, D), 0.7, 4.0, ((1, 8),), jnp.float32)
    query_branch = scatter_about(splits[3], (SEQLEN, D), 1.0, 6.0, ((0, 32), (1, 8)))
    key_branch = scatter_about(splits[4], (SEQLEN, D), 1.0, 6.0, ((0, 32), (1, 8)))
    decay_rate = draw_decay_rate(jax.random.fold_in(splits[11], 71), 0)
    weight_first = scatter_about(splits[6], (FEAT, FH), FEAT ** -0.5, 1.0, (), jnp.float32)
    weight_second = scatter_about(splits[7], (FH, FH), FH ** -0.5, 0.75, (), jnp.float32)
    weight_third = scatter_about(splits[8], (FH, D), FH ** -0.5, 0.75, ((1, 8),), jnp.float32)
    skip_gain = scatter_about(splits[9], (D,), 1.0, 4.0, ((0, 8),), jnp.float32)
    cotangent = scatter_about(splits[10], (SEQLEN, D), 1.0, 6.0, ((0, 32), (1, 8)))
    return {"tokens": tokens, "embed_table": embed_table, "short_conv": short_conv, "query_branch": query_branch, "key_branch": key_branch, "decay_rate": decay_rate, "weight_first": weight_first, "weight_second": weight_second, "weight_third": weight_third, "skip_gain": skip_gain, "cotangent": cotangent}


highest = lax.Precision.HIGHEST
two_pi = 2.0 * math.pi

def features(positions, length):
    frequency = 2 ** jnp.arange(BANDS, dtype=jnp.int32) + 1
    phases = positions[:, None] * frequency[None, :] % length
    angles = phases.astype(jnp.float32) * (two_pi / length)
    ramp_col = positions.astype(jnp.float32)[:, None] / length
    return jnp.concatenate([ramp_col, jnp.cos(angles), jnp.sin(angles)], axis=1)

def filter_forward(positions, length, weight_first, weight_second, weight_third, decay_rate):
    embedding = features(positions, length)
    pre_one = jnp.dot(embedding, weight_first, precision=highest, preferred_element_type=jnp.float32)
    act_one = jnp.sin(pre_one)
    pre_two = jnp.dot(act_one, weight_second, precision=highest, preferred_element_type=jnp.float32)
    act_two = jnp.sin(pre_two)
    shaped = jnp.dot(act_two, weight_third, precision=highest, preferred_element_type=jnp.float32)
    scaling = jnp.sqrt(jnp.expm1(-2.0 * decay_rate) / jnp.expm1(-2.0 * length * decay_rate))
    window = scaling[None, :] * jnp.exp(-decay_rate[None, :] * positions.astype(jnp.float32)[:, None])
    return (shaped * window, (window, embedding, pre_one, act_one, pre_two, act_two))

def filter_head(grad_filter, saved_acts, weight_third):
    window, embedding, pre_one, act_one, pre_two, act_two = saved_acts
    grad_shaped = grad_filter * window
    grad_third = jnp.dot(act_two.T, grad_shaped, precision=highest, preferred_element_type=jnp.float32)
    grad_act_two = jnp.dot(grad_shaped, weight_third.T, precision=highest, preferred_element_type=jnp.float32)
    return (grad_third, grad_act_two)

def filter_tail(grad_act_two, saved_acts, weight_second):
    window, embedding, pre_one, act_one, pre_two, act_two = saved_acts
    grad_pre_two = grad_act_two * jnp.cos(pre_two)
    grad_second = jnp.dot(act_one.T, grad_pre_two, precision=highest, preferred_element_type=jnp.float32)
    grad_act_one = jnp.dot(grad_pre_two, weight_second.T, precision=highest, preferred_element_type=jnp.float32)
    grad_pre_one = grad_act_one * jnp.cos(pre_one)
    grad_first = jnp.dot(embedding.T, grad_pre_one, precision=highest, preferred_element_type=jnp.float32)
    return (grad_first, grad_second)

def reference(tokens, embed_table, short_conv, query_branch, key_branch, decay_rate, weight_first, weight_second, weight_third, skip_gain, cotangent):
    length = tokens.shape[0]
    points = 2 * length
    inv_root = 1.0 / math.sqrt(length)
    vocab_size = embed_table.shape[0]
    embedded = embed_table[tokens].astype(jnp.float32)
    padded = jnp.concatenate([jnp.zeros((2, embedded.shape[1]), jnp.float32), embedded], axis=0)
    value_branch = short_conv[0] * padded[2:] + short_conv[1] * padded[1:-1] + short_conv[2] * padded[:-2]
    keyed_value = key_branch.astype(jnp.float32) * value_branch
    query_rows = query_branch.astype(jnp.float32)
    grad_out = cotangent.astype(jnp.float32)
    positions = jnp.arange(length, dtype=jnp.int32)
    filter_rows, saved_acts = filter_forward(positions, length, weight_first, weight_second, weight_third, decay_rate)
    grad_z = grad_out * query_rows
    spec_keyed = jnp.fft.rfft(keyed_value, n=points, axis=0)
    spec_filter = jnp.fft.rfft(filter_rows, n=points, axis=0)
    spec_grad = jnp.fft.rfft(grad_z, n=points, axis=0)
    convolved = jnp.fft.irfft(spec_keyed * spec_filter, n=points, axis=0)[:length]
    back_keyed = jnp.fft.irfft(jnp.conj(spec_filter) * spec_grad, n=points, axis=0)[:length]
    grad_filter = jnp.fft.irfft(jnp.conj(spec_keyed) * spec_grad, n=points, axis=0)[:length]
    inner_sum = convolved + skip_gain * keyed_value
    operator_out = (query_rows * inner_sum).astype(jnp.bfloat16)
    grad_query = (grad_out * inner_sum).astype(jnp.bfloat16)
    grad_keyed = back_keyed + skip_gain * grad_z
    grad_key = (grad_keyed * value_branch).astype(jnp.bfloat16)
    grad_value = grad_keyed * key_branch.astype(jnp.float32)
    grad_short = jnp.stack([lax.optimization_barrier(jnp.sum(grad_value * padded[2 - offset:2 - offset + length], axis=0)) for offset in range(3)]) * inv_root
    grad_skip = lax.optimization_barrier(jnp.sum(grad_z * keyed_value, axis=0)) * inv_root
    grad_embed = jnp.zeros((vocab_size, embedded.shape[1]), jnp.float32)
    for offset in range(3):
        grad_embed = grad_embed + jax.ops.segment_sum(short_conv[offset] * grad_value[offset:], tokens[:length - offset], num_segments=vocab_size)
    grad_embed = grad_embed * inv_root
    grad_third, grad_act_two = filter_head(grad_filter, saved_acts, weight_third)
    grad_first, grad_second = filter_tail(grad_act_two, saved_acts, weight_second)
    return (operator_out, grad_query, grad_key, grad_embed, grad_short, grad_skip, grad_first * inv_root, grad_second * inv_root, grad_third * inv_root)
```

```python
import math

import jax
import jax.numpy as jnp
import numpy as np
from jax import lax
from jax.sharding import PartitionSpec as P

BANDS = 16

high = lax.Precision.HIGH
highest = lax.Precision.HIGHEST
two_pi = 2.0 * math.pi


def transform_tables(parts, rows, lanes):
    length = parts * rows
    freq = 4 * np.arange(parts, dtype=np.int64) + 1
    phase = freq[:, None] * np.arange(parts, dtype=np.int64)[None, :] % (4 * parts)
    angle = two_pi * phase / (4 * parts)
    stage = np.concatenate([np.cos(angle), -np.sin(angle)], axis=0)
    first = np.kron(stage, np.eye(lanes))
    turn = freq[:, None] * np.arange(rows, dtype=np.int64)[None, :] % (4 * length)
    turn = two_pi * turn / (4 * length)
    inner = np.arange(rows, dtype=np.int64)
    inner = two_pi * (inner[:, None] * inner[None, :] % rows) / rows
    single = lambda table: np.asarray(table, np.float32)
    return (
        single(first),
        single(np.cos(turn)),
        single(np.sin(turn)),
        single(np.concatenate([np.cos(inner), np.sin(inner)], axis=1)),
    )


def feature_table(length):
    positions = np.arange(length, dtype=np.int64)
    frequency = 2 ** np.arange(BANDS, dtype=np.int64) + 1
    phases = frequency[:, None] * positions[None, :] % length
    angles = two_pi * phases / length
    table = np.concatenate([positions[None, :] / length, np.cos(angles), np.sin(angles)], axis=0)
    return np.asarray(table, np.float32)


def dot3(left, right):
    return jnp.dot(left, right, precision=high, preferred_element_type=jnp.float32)


def shift_back(block, lanes, steps):
    before = jnp.concatenate([jnp.zeros_like(block[:lanes]), block[:-lanes]], axis=0)
    return jnp.concatenate([before[:, -steps:], block[:, :-steps]], axis=1)


def shift_ahead(block, lanes, steps):
    after = jnp.concatenate([block[lanes:], jnp.zeros_like(block[:lanes])], axis=0)
    return jnp.concatenate([block[:, steps:], after[:, :steps]], axis=1)


def per_device(
    tokens,
    embed_table,
    short_conv,
    query_branch,
    key_branch,
    decay_rate,
    weight_first,
    weight_second,
    weight_third,
    skip_gain,
    cotangent,
):
    parts = lax.axis_size("seq")
    groups = lax.axis_size("chan")
    seq_index = lax.axis_index("seq")
    rows, width = query_branch.shape
    lanes = width // parts
    length = rows * parts
    inv_root = 1.0 / math.sqrt(length)
    vocab_size = embed_table.shape[0]
    hidden = weight_first.shape[1]
    own = seq_index * lanes

    query_rows = query_branch.astype(jnp.float32)
    key_rows = key_branch.astype(jnp.float32)
    grad_out = cotangent.astype(jnp.float32)
    key_cols = key_rows.T.reshape(parts, lanes, rows)
    grad_cols = (grad_out * query_rows).T.reshape(parts, lanes, rows)
    token_cols = jnp.broadcast_to(tokens.astype(jnp.float32)[None, None, :], (parts, 1, rows))
    packed = jnp.concatenate([key_cols, grad_cols, token_cols], axis=1)
    packed = lax.all_to_all(packed, "seq", 0, 0, tiled=True)
    key_all = packed[:, :lanes].reshape(parts * lanes, rows)
    grad_z = packed[:, lanes : 2 * lanes].reshape(parts * lanes, rows)
    token_all = packed[:, 2 * lanes].astype(jnp.int32)

    embed_own = lax.dynamic_slice_in_dim(embed_table, own, lanes, axis=1)
    short_own = lax.dynamic_slice_in_dim(short_conv, own, lanes, axis=1)
    decay_own = lax.dynamic_slice_in_dim(decay_rate, own, lanes, axis=0)
    skip_own = lax.dynamic_slice_in_dim(skip_gain, own, lanes, axis=0)
    third_own = lax.dynamic_slice_in_dim(weight_third, own, lanes, axis=1)
    by_row = lambda values: jnp.tile(values, parts)[:, None]

    vocab_ids = jnp.arange(vocab_size, dtype=jnp.int32)
    match = token_all[None] == vocab_ids[:, None, None]
    embedded = jnp.einsum(
        "wc,wsp->scp", embed_own, match.astype(jnp.bfloat16), preferred_element_type=jnp.float32
    ).reshape(parts * lanes, rows)
    lagged = [embedded, shift_back(embedded, lanes, 1), shift_back(embedded, lanes, 2)]
    value = sum(by_row(short_own[lag]) * lagged[lag] for lag in range(3))
    keyed = key_all * value

    features = jnp.asarray(feature_table(length))
    pre_one = dot3(weight_first.T, features)
    act_one = jnp.sin(pre_one)
    pre_two = dot3(weight_second.T, act_one)
    act_two = jnp.sin(pre_two)
    shaped = dot3(third_own.T, act_two)
    scaling = jnp.sqrt(jnp.expm1(-2.0 * decay_own) / jnp.expm1(-2.0 * length * decay_own))
    positions = jnp.arange(length, dtype=jnp.int32).astype(jnp.float32)
    window = scaling[:, None] * jnp.exp(-decay_own[:, None] * positions[None, :])
    filter_flat = shaped * window
    filter_rows = (
        filter_flat.reshape(lanes, parts, rows).transpose(1, 0, 2).reshape(parts * lanes, rows)
    )

    first, turn_cos, turn_sin, inner = (
        jnp.asarray(table) for table in transform_tables(parts, rows, lanes)
    )
    half = parts * lanes
    turn_cos = jnp.repeat(turn_cos, lanes, axis=0)
    turn_sin = jnp.repeat(turn_sin, lanes, axis=0)

    def forward(block):
        stage = dot3(first, block)
        real, imag = stage[:half], stage[half:]
        turned = jnp.concatenate(
            [real * turn_cos + imag * turn_sin, imag * turn_cos - real * turn_sin], axis=0
        )
        both = dot3(turned, inner)
        return (
            both[:half, :rows] + both[half:, rows:],
            both[half:, :rows] - both[:half, rows:],
        )

    def inverse(spectrum):
        both = dot3(jnp.concatenate(spectrum, axis=0), inner)
        real = both[:half, :rows] - both[half:, rows:]
        imag = both[half:, :rows] + both[:half, rows:]
        turned = jnp.concatenate(
            [real * turn_cos - imag * turn_sin, imag * turn_cos + real * turn_sin], axis=0
        )
        return dot3(first.T, turned) * (1.0 / length)

    keyed_spec, filter_spec, grad_spec = forward(keyed), forward(filter_rows), forward(grad_z)

    def times(left, right):
        return (left[0] * right[0] - left[1] * right[1], left[0] * right[1] + left[1] * right[0])

    def against(left, right):
        return (left[0] * right[0] + left[1] * right[1], left[0] * right[1] - left[1] * right[0])

    convolved = inverse(times(keyed_spec, filter_spec))
    back_keyed = inverse(against(filter_spec, grad_spec))
    grad_filter = inverse(against(keyed_spec, grad_spec))

    skip_rows = by_row(skip_own)
    inner_sum = convolved + skip_rows * keyed
    grad_keyed = back_keyed + skip_rows * grad_z
    grad_value = grad_keyed * key_all

    def per_channel(block):
        return jnp.sum(block.reshape(parts, lanes, rows), axis=(0, 2))

    short_part = jnp.stack([per_channel(grad_value * lagged[lag]) for lag in range(3)])
    skip_part = per_channel(grad_z * keyed)
    scattered = (
        by_row(short_own[0]) * grad_value
        + by_row(short_own[1]) * shift_ahead(grad_value, lanes, 1)
        + by_row(short_own[2]) * shift_ahead(grad_value, lanes, 2)
    )
    upper = lax.reduce_precision(scattered, 8, 7)
    lower = (scattered - upper).astype(jnp.bfloat16)
    upper = upper.astype(jnp.bfloat16)
    both = jnp.concatenate(
        [upper.reshape(parts, lanes, rows), lower.reshape(parts, lanes, rows)], axis=1
    )
    embed_part = jnp.einsum(
        "wsp,scp->wc", match.astype(jnp.bfloat16), both, preferred_element_type=jnp.float32
    )
    embed_part = embed_part[:, :lanes] + embed_part[:, lanes:]

    grad_flat = grad_filter.reshape(parts, lanes, rows).transpose(1, 0, 2).reshape(lanes, length)
    grad_shaped = grad_flat * window
    dot_last = lambda left, right: lax.dot_general(
        left, right, (((1,), (1,)), ((), ())), precision=high, preferred_element_type=jnp.float32
    )
    third_part = dot_last(act_two, grad_shaped)
    grad_pre_two = dot3(third_own, grad_shaped) * jnp.cos(pre_two)
    second_part = dot_last(act_one, grad_pre_two)
    grad_pre_one = dot3(weight_second, grad_pre_two) * jnp.cos(pre_one)
    first_part = dot_last(features, grad_pre_one)

    summed = jnp.concatenate([second_part.reshape(-1), first_part.reshape(-1)])
    share = -(-summed.shape[0] // parts)
    summed = jnp.pad(summed, (0, share * parts - summed.shape[0])).reshape(parts, share)
    spread = lambda values: jnp.broadcast_to(values.reshape(1, -1), (parts, values.size))
    small = jnp.concatenate(
        [
            embed_part.reshape(parts, -1),
            spread(short_part),
            spread(skip_part),
            spread(third_part),
            summed,
        ],
        axis=1,
    )
    small_rows = -(-small.shape[1] // rows)
    small = jnp.pad(small, ((0, 0), (0, small_rows * rows - small.shape[1])))
    packed = jnp.concatenate(
        [
            inner_sum.reshape(parts, lanes, rows),
            grad_keyed.reshape(parts, lanes, rows),
            small.reshape(parts, small_rows, rows),
        ],
        axis=1,
    )
    packed = lax.all_to_all(packed, "seq", 0, 0, tiled=True)
    inner_own = packed[:, :lanes].reshape(width, rows).T
    grad_own = packed[:, lanes : 2 * lanes].reshape(width, rows).T
    small = packed[:, 2 * lanes :].reshape(parts, -1)

    own_vocab = vocab_size // parts
    cut = np.cumsum([own_vocab * lanes, 3 * lanes, lanes, hidden * lanes, share])
    grad_embed = small[:, : cut[0]].reshape(parts, own_vocab, lanes).transpose(1, 0, 2)
    grad_embed = grad_embed.reshape(own_vocab, width) * inv_root
    grad_short = small[:, cut[0] : cut[1]].reshape(parts, 3, lanes).transpose(1, 0, 2)
    grad_short = grad_short.reshape(3, width) * inv_root
    grad_skip = small[:, cut[1] : cut[2]].reshape(width) * inv_root
    grad_third = small[:, cut[2] : cut[3]].reshape(parts, hidden, lanes).transpose(1, 0, 2)
    grad_third = grad_third.reshape(hidden, width) * inv_root

    partial = jnp.sum(small[:, cut[3] : cut[4]], axis=0)
    padded = -(-share // 128) * 128
    partial = jnp.pad(partial, (0, padded - share)).reshape(1, padded // 128, 128)
    partial = jnp.broadcast_to(partial, (parts * groups,) + partial.shape[1:])
    partial = lax.all_to_all(partial, ("seq", "chan"), 0, 0, tiled=True)
    total = jnp.sum(partial.reshape(parts, groups, padded), axis=1)[:, :share].reshape(-1)
    count = hidden * hidden
    grad_second = total[:count].reshape(hidden, hidden) * inv_root
    grad_first = total[count : count + first_part.size].reshape(first_part.shape) * inv_root

    lookup_ids = token_all.reshape(-1)
    start = seq_index * rows
    padded_ids = jnp.concatenate([jnp.full((2,), -1, jnp.int32), lookup_ids])
    window_ids = lax.dynamic_slice_in_dim(padded_ids, start, rows + 2)
    lookup = (window_ids[:, None] == vocab_ids[None, :]).astype(jnp.bfloat16)
    embedded = jnp.dot(lookup, embed_table, preferred_element_type=jnp.float32)
    value_rows = (
        short_conv[0] * embedded[2:]
        + short_conv[1] * embedded[1:-1]
        + short_conv[2] * embedded[:-2]
    )
    operator_out = (query_rows * inner_own).astype(jnp.bfloat16)
    grad_query = (grad_out * inner_own).astype(jnp.bfloat16)
    grad_key = (grad_own * value_rows).astype(jnp.bfloat16)
    return (
        operator_out,
        grad_query,
        grad_key,
        grad_embed,
        grad_short,
        grad_skip,
        grad_first,
        grad_second,
        grad_third,
    )


def solution(mesh):
    in_specs = (
        P("seq"),
        P(None, "chan"),
        P(None, "chan"),
        P("seq", "chan"),
        P("seq", "chan"),
        P("chan"),
        P(),
        P(),
        P(None, "chan"),
        P("chan"),
        P("seq", "chan"),
    )
    out_specs = (
        P("seq", "chan"),
        P("seq", "chan"),
        P("seq", "chan"),
        P("seq", "chan"),
        P(None, "chan"),
        P("chan"),
        P(),
        P(),
        P(None, "chan"),
    )
    return jax.shard_map(
        per_device, mesh=mesh, in_specs=in_specs, out_specs=out_specs, check_vma=False
    )
```

```python
import math

import jax
import jax.numpy as jnp
import numpy as np
from jax import lax
from jax.experimental import pallas as pl
from jax.experimental.pallas import tpu as pltpu
from jax.sharding import PartitionSpec as P

BANDS = 16
STEPS = 4

two_pi = 2.0 * math.pi
f32 = jnp.float32
bf16 = jnp.bfloat16


def halves(table):
    upper = np.asarray(np.asarray(table, np.float32), bf16)
    lower = np.asarray(np.asarray(table, np.float32) - np.asarray(upper, np.float32), bf16)
    return upper, lower


def transform_tables(parts, rows, lanes):
    length = parts * rows
    freq = 4 * np.arange(parts, dtype=np.int64) + 1
    phase = freq[:, None] * np.arange(parts, dtype=np.int64)[None, :] % (4 * parts)
    angle = two_pi * phase / (4 * parts)
    stage = np.concatenate([np.cos(angle), -np.sin(angle)], axis=0)
    first = np.kron(stage, np.eye(lanes))
    turn = freq[:, None] * np.arange(rows, dtype=np.int64)[None, :] % (4 * length)
    turn = two_pi * turn / (4 * length)
    inner = np.arange(rows, dtype=np.int64)
    inner = two_pi * (inner[:, None] * inner[None, :] % rows) / rows
    inner = np.concatenate([np.cos(inner), np.sin(inner)], axis=1)
    turns = np.stack([np.cos(turn), np.sin(turn)]).astype(np.float32)
    return halves(first) + halves(first.T) + halves(inner), turns


def feature_table(length):
    positions = np.arange(length, dtype=np.int64)
    frequency = 2 ** np.arange(BANDS, dtype=np.int64) + 1
    phases = frequency[:, None] * positions[None, :] % length
    angles = two_pi * phases / length
    table = np.concatenate([positions[None, :] / length, np.cos(angles), np.sin(angles)], axis=0)
    spare = -table.shape[0] % 8
    return np.asarray(np.pad(table, ((0, spare), (0, 0))), np.float32)


def split(block):
    upper = block.astype(bf16)
    return upper, (block - upper.astype(f32)).astype(bf16)


def dot(left, right):
    return jnp.dot(left, right, preferred_element_type=f32)


def dot_last(left, right):
    return lax.dot_general(left, right, (((1,), (1,)), ((), ())), preferred_element_type=f32)


def product(left, right, by=dot):
    return by(left[0], right[0]) + (by(left[1], right[0]) + by(left[0], right[1]))


def product_last(left, right):
    return product(left, right, dot_last)


def sine_cosine(angle):
    turns = jnp.floor(angle * (2.0 / math.pi) + 0.5)
    rest = angle - turns * 1.5703125
    rest = rest - turns * 4.837512969970703125e-4
    rest = rest - turns * 7.54978995489188216e-8
    square = rest * rest
    sine = ((-1.9515295891e-4 * square + 8.3321608736e-3) * square - 1.6666654611e-1) * square
    sine = sine * rest + rest
    cosine = (2.443315711809948e-5 * square - 1.388731625493765e-3) * square
    cosine = (cosine + 4.166664568298827e-2) * square * square - 0.5 * square + 1.0
    quarter = turns.astype(jnp.int32)
    odd = (quarter & 1) == 1
    sine, cosine = jnp.where(odd, cosine, sine), jnp.where(odd, sine, cosine)
    sine = jnp.where((quarter & 2) == 2, -sine, sine)
    cosine = jnp.where(((quarter + 1) & 2) == 2, -cosine, cosine)
    return sine, cosine


def spread_turns(turn_ref, lanes):
    def one(table):
        parts, rows = table.shape
        wide = jnp.broadcast_to(table[:, None, :], (parts, lanes, rows))
        return wide.reshape(parts * lanes, rows)

    return one(turn_ref[0]), one(turn_ref[1])


def forward(block, first, inner, turns):
    half, rows = block.shape
    stage = product(first, split(block))
    real, imag = stage[:half], stage[half:]
    turned_real = real * turns[0] + imag * turns[1]
    turned_imag = imag * turns[0] - real * turns[1]
    along = product(split(turned_real), inner)
    across = product(split(turned_imag), inner)
    return along[:, :rows] + across[:, rows:], across[:, :rows] - along[:, rows:]


def inverse(spectrum, first_back, inner, turns, length):
    half, rows = spectrum[0].shape
    along = product(split(spectrum[0]), inner)
    across = product(split(spectrum[1]), inner)
    real = along[:, :rows] - across[:, rows:]
    imag = across[:, :rows] + along[:, rows:]
    turned_real = real * turns[0] - imag * turns[1]
    turned_imag = imag * turns[0] + real * turns[1]
    turned = jnp.concatenate([turned_real, turned_imag], axis=0)
    return product(first_back, split(turned)) * (1.0 / length)


def times(left, right):
    return left[0] * right[0] - left[1] * right[1], left[0] * right[1] + left[1] * right[0]


def against(left, right):
    return left[0] * right[0] + left[1] * right[1], left[0] * right[1] - left[1] * right[0]


def shift_back(block, lanes, steps):
    rolled = pltpu.roll(block, steps, 1)
    before = jnp.concatenate([jnp.zeros_like(rolled[:lanes]), rolled[:-lanes]], axis=0)
    column = lax.broadcasted_iota(jnp.int32, block.shape, 1)
    return jnp.where(column < steps, before, rolled)


def shift_ahead(block, lanes, steps):
    width = block.shape[1]
    rolled = pltpu.roll(block, width - steps, 1)
    after = jnp.concatenate([rolled[lanes:], jnp.zeros_like(rolled[:lanes])], axis=0)
    column = lax.broadcasted_iota(jnp.int32, block.shape, 1)
    return jnp.where(column >= width - steps, after, rolled)


def pack_kernel(key_ref, query_ref, cotangent_ref, token_ref, out_ref):
    parts = out_ref.shape[0]
    rows = key_ref.shape[0]
    lanes = key_ref.shape[1] // parts
    key_cols = key_ref[...].astype(f32).T
    grad_cols = (cotangent_ref[...].astype(f32) * query_ref[...].astype(f32)).T
    place = 0
    for block in (key_cols, grad_cols):
        for start in range(0, rows, 128):
            piece = block[:, start : start + 128].reshape(parts, lanes, 128)
            out_ref[:, place : place + lanes, :] = piece
            place += lanes
    ids = token_ref[...].astype(f32)
    out_ref[:, place : place + lanes, :] = jnp.broadcast_to(ids[None], (parts, lanes, 128))


def front_kernel(
    feature_ref,
    first_ref,
    second_ref,
    third_ref,
    param_ref,
    fwd_hi,
    fwd_lo,
    in_hi,
    in_lo,
    turn_ref,
    act_one_ref,
    cos_one_ref,
    act_two_ref,
    cos_two_ref,
    window_ref,
    spec_ref,
    filter_ref,
):
    step = pl.program_id(0)
    lanes = third_ref.shape[0]
    half, rows = window_ref.shape
    length = half // lanes * rows
    block = feature_ref.shape[1]
    pre_one = product(split(first_ref[...]), split(feature_ref[...]))
    act_one, cos_one = sine_cosine(pre_one)
    act_one_ref[...] = act_one
    cos_one_ref[...] = cos_one
    pre_two = product(split(second_ref[...]), split(act_one))
    act_two, cos_two = sine_cosine(pre_two)
    act_two_ref[...] = act_two
    cos_two_ref[...] = cos_two
    shaped = product(split(third_ref[...]), split(act_two))
    count = block // rows
    for part in range(count):
        place = pl.multiple_of((step * count + part) * lanes, lanes)
        filter_ref[pl.ds(place, lanes), :] = shaped[:, part * rows : (part + 1) * rows]

    @pl.when(step == STEPS - 1)
    def _():
        row = lax.broadcasted_iota(jnp.int32, (half, rows), 0)
        column = lax.broadcasted_iota(jnp.int32, (half, rows), 1)
        position = (row // lanes * rows + column).astype(f32)
        window = param_ref[:, 1:2] * jnp.exp(-param_ref[:, 0:1] * position)
        window_ref[...] = window
        first = (fwd_hi[...], fwd_lo[...])
        inner = (in_hi[...], in_lo[...])
        turns = spread_turns(turn_ref, lanes)
        real, imag = forward(filter_ref[...] * window, first, inner, turns)
        spec_ref[0] = real
        spec_ref[1] = imag


def middle_kernel(
    packed_ref,
    embed_ref,
    param_ref,
    window_ref,
    spec_ref,
    fwd_hi,
    fwd_lo,
    back_hi,
    back_lo,
    in_hi,
    in_lo,
    turn_ref,
    feature_ref,
    act_one_ref,
    cos_one_ref,
    act_two_ref,
    cos_two_ref,
    second_ref,
    third_ref,
    out_ref,
    embedded_ref,
    shaped_ref,
    pieces_ref,
    small_ref,
    third_acc,
    second_acc,
    first_acc,
):
    step = pl.program_id(0)
    parts = packed_ref.shape[0]
    half, rows = window_ref.shape
    lanes = half // parts
    length = parts * rows
    vocab = embed_ref.shape[1]
    hidden = second_ref.shape[0]

    @pl.when(step == 0)
    def _():
        third_acc[...] = jnp.zeros_like(third_acc)
        second_acc[...] = jnp.zeros_like(second_acc)
        first_acc[...] = jnp.zeros_like(first_acc)
        small_ref[...] = jnp.zeros_like(small_ref)
        names = lax.broadcasted_iota(jnp.int32, (vocab, rows), 0).astype(f32)
        table = embed_ref[...]

        def matches(part):
            ids = packed_ref[part, 4 * lanes : 4 * lanes + 2, :]
            ids = jnp.concatenate([ids[0:1], ids[1:2]], axis=1)
            return jnp.where(names == ids, 1.0, 0.0).astype(bf16)

        def look_up(part, carry):
            place = pl.multiple_of(part * lanes, lanes)
            embedded_ref[pl.ds(place, lanes), :] = dot(table, matches(part))
            return carry

        lax.fori_loop(0, parts, look_up, 0, unroll=4)

        def received(place):
            pair = [
                packed_ref[:, place + off * lanes : place + (off + 1) * lanes, :].reshape(half, 128)
                for off in range(2)
            ]
            return jnp.concatenate(pair, axis=1)

        key_all = received(0)
        grad_z = received(2 * lanes)
        embedded = embedded_ref[...]
        lagged = [embedded, shift_back(embedded, lanes, 1), shift_back(embedded, lanes, 2)]
        gains = [param_ref[:, 3 + lag : 4 + lag] for lag in range(3)]
        value = gains[0] * lagged[0] + gains[1] * lagged[1] + gains[2] * lagged[2]
        keyed = key_all * value
        first = (fwd_hi[...], fwd_lo[...])
        first_back = (back_hi[...], back_lo[...])
        inner = (in_hi[...], in_lo[...])
        turns = spread_turns(turn_ref, lanes)
        keyed_spec = forward(keyed, first, inner, turns)
        grad_spec = forward(grad_z, first, inner, turns)
        filter_spec = (spec_ref[0], spec_ref[1])
        back = lambda spectrum: inverse(spectrum, first_back, inner, turns, length)
        shaped_ref[...] = back(against(keyed_spec, grad_spec)) * window_ref[...]
        skip_gain = param_ref[:, 2:3]
        inner_sum = back(times(keyed_spec, filter_spec)) + skip_gain * keyed
        grad_keyed = back(against(filter_spec, grad_spec)) + skip_gain * grad_z
        place = 0
        for block in (inner_sum, grad_keyed):
            for start in range(0, rows, 128):
                piece = block[:, start : start + 128].reshape(parts, lanes, 128)
                out_ref[:, place : place + lanes, :] = piece
                place += lanes
        grad_value = grad_keyed * key_all

        def per_channel(block):
            return jnp.sum(jnp.sum(block.reshape(parts, lanes, rows), axis=0), axis=1, keepdims=True)

        for lag in range(3):
            small_ref[:, 16 + lag : 17 + lag] = per_channel(grad_value * lagged[lag])
        small_ref[:, 19:20] = per_channel(grad_z * keyed)
        scattered = gains[0] * grad_value
        for lag in (1, 2):
            scattered = scattered + gains[lag] * shift_ahead(grad_value, lanes, lag)
        upper, lower = split(scattered)
        both = (upper.reshape(parts, lanes, rows), lower.reshape(parts, lanes, rows))
        pieces_ref[...] = jnp.concatenate(both, axis=1)

        def collect(part, total):
            return total + dot_last(pieces_ref[part], matches(part))

        total = lax.fori_loop(0, parts, collect, jnp.zeros((2 * lanes, vocab), f32), unroll=4)
        embed_part = total[:lanes] + total[lanes:]
        share = vocab // parts
        out_ref[:, 4 * lanes :, :] = jnp.zeros((parts, lanes, 128), f32)
        for part in range(parts):
            own = embed_part[:, part * share : (part + 1) * share]
            out_ref[part, 4 * lanes :, 0:share] = own

    block = feature_ref.shape[1]
    count = block // rows
    pieces = []
    for part in range(count):
        place = pl.multiple_of((step * count + part) * lanes, lanes)
        pieces.append(shaped_ref[pl.ds(place, lanes), :])
    grad_shaped = split(jnp.concatenate(pieces, axis=1))
    act_two = split(act_two_ref[...])
    third_acc[...] += product_last(grad_shaped, act_two)
    grad_pre_two = product(split(third_ref[...]), grad_shaped) * cos_two_ref[...]
    grad_pre_two = split(grad_pre_two)
    second_acc[...] += product_last(split(act_one_ref[...]), grad_pre_two)
    grad_pre_one = product(split(second_ref[...]), grad_pre_two) * cos_one_ref[...]
    first_acc[...] += product_last(split(grad_pre_one), split(feature_ref[...]))

    @pl.when(step == STEPS - 1)
    def _():
        spare = jnp.zeros((hidden, hidden - first_acc.shape[1]), f32)
        joined = (second_acc[...], first_acc[...], spare)
        hidden_part = jnp.concatenate(joined, axis=1)
        cut = 2 * hidden // 4
        stacked = [hidden_part[:, cut * i : cut * (i + 1)] for i in range(4)]
        stacked = jnp.concatenate(stacked, axis=0)
        low = 4 * lanes
        out_ref[:, low:, cut : 2 * cut] = stacked.reshape(parts, lanes, cut)
        third_part = jnp.broadcast_to(third_acc[...][None], (parts, lanes, hidden))
        out_ref[:, low:, 128 - hidden : 128] = third_part
        tail = jnp.broadcast_to(small_ref[:, 16:20][None], (parts, lanes, 4))
        out_ref[:, low:, 16:20] = tail


def finish_kernel(
    packed_ref,
    query_ref,
    cotangent_ref,
    value_ref,
    out_ref,
    grad_query_ref,
    grad_key_ref,
    embed_ref,
    short_ref,
    skip_ref,
    third_ref,
):
    parts = packed_ref.shape[0]
    width = query_ref.shape[1]
    rows = query_ref.shape[0]
    lanes = width // parts
    inv_root = 1.0 / math.sqrt(parts * rows)

    def received(place):
        tile = lambda at: packed_ref[:, at : at + lanes, :].reshape(width, 128)
        return jnp.concatenate([tile(place).T, tile(place + lanes).T], axis=0)

    inner_sum = received(0)
    out_ref[...] = (query_ref[...].astype(f32) * inner_sum).astype(bf16)
    grad_query_ref[...] = (cotangent_ref[...].astype(f32) * inner_sum).astype(bf16)
    grad_key_ref[...] = (received(2 * lanes) * value_ref[...]).astype(bf16)
    small = packed_ref[:, 4 * lanes :, :].reshape(width, 128).T * inv_root
    embed_ref[...] = small[0 : embed_ref.shape[0]]
    short_ref[...] = small[16:19]
    skip_ref[...] = small[19:20]
    third_ref[...] = small[128 - third_ref.shape[0] :]


def per_device(
    tokens,
    embed_table,
    short_conv,
    query_branch,
    key_branch,
    decay_rate,
    weight_first,
    weight_second,
    weight_third,
    skip_gain,
    cotangent,
):
    parts = lax.axis_size("seq")
    groups = lax.axis_size("chan")
    seq_index = lax.axis_index("seq")
    rows, width = query_branch.shape
    lanes = width // parts
    half = parts * lanes
    length = rows * parts
    inv_root = 1.0 / math.sqrt(length)
    vocab_size = embed_table.shape[0]
    hidden = weight_first.shape[1]
    own = seq_index * lanes
    shape = jax.ShapeDtypeStruct
    chunk = (parts, 5 * lanes, 128)
    whole = pl.BlockSpec(memory_space=pltpu.VMEM)

    packed = pl.pallas_call(
        pack_kernel,
        out_shape=shape(chunk, f32),
        in_specs=[whole] * 4,
        out_specs=whole,
        name="pack",
    )(key_branch, query_branch, cotangent, jnp.pad(tokens.reshape(2, 128), ((0, lanes - 2), (0, 0))))
    packed = lax.all_to_all(packed, "seq", 0, 0, tiled=True)

    embed_own = lax.dynamic_slice_in_dim(embed_table, own, lanes, axis=1).T
    short_own = lax.dynamic_slice_in_dim(short_conv, own, lanes, axis=1)
    decay_own = lax.dynamic_slice_in_dim(decay_rate, own, lanes, axis=0)
    skip_own = lax.dynamic_slice_in_dim(skip_gain, own, lanes, axis=0)
    third_own = lax.dynamic_slice_in_dim(weight_third, own, lanes, axis=1)
    scaling = jnp.sqrt(jnp.expm1(-2.0 * decay_own) / jnp.expm1(-2.0 * length * decay_own))
    params = [decay_own, scaling, skip_own, short_own[0], short_own[1], short_own[2]]
    params = jnp.tile(jnp.stack(params + [skip_own, skip_own], axis=1), (parts, 1))

    (fwd_hi, fwd_lo, back_hi, back_lo, in_hi, in_lo), turns = transform_tables(parts, rows, lanes)
    features = jnp.asarray(feature_table(length))
    feats = features.shape[0]
    first_t = jnp.pad(weight_first.T, ((0, 0), (0, feats - weight_first.shape[0])))
    block = length // STEPS
    still = lambda array: pl.BlockSpec(array.shape, lambda i: (0,) * array.ndim)
    moving = lambda count: pl.BlockSpec((count, block), lambda i: (0, i))

    act = shape((hidden, length), f32)
    window_shape, spec_shape = shape((half, rows), f32), shape((2, half, rows), f32)
    second_t, third_t = weight_second.T, third_own.T
    act_one, cos_one, act_two, cos_two, window, spec = pl.pallas_call(
        front_kernel,
        out_shape=(act, act, act, act, window_shape, spec_shape),
        grid=(STEPS,),
        in_specs=[moving(feats)]
        + [still(a) for a in (first_t, second_t, third_t, params, fwd_hi, fwd_lo, in_hi, in_lo, turns)],
        out_specs=[moving(hidden)] * 4 + [still(window_shape), still(spec_shape)],
        scratch_shapes=[pltpu.VMEM((half, rows), f32)],
        name="front",
    )(features, first_t, second_t, third_t, params, fwd_hi, fwd_lo, in_hi, in_lo, turns)

    operands = (packed, embed_own, params, window, spec, fwd_hi, fwd_lo, back_hi, back_lo, in_hi, in_lo, turns)
    sent = pl.pallas_call(
        middle_kernel,
        out_shape=shape(chunk, f32),
        grid=(STEPS,),
        in_specs=[still(a) for a in operands]
        + [moving(feats)]
        + [moving(hidden)] * 4
        + [still(weight_second), still(third_own)],
        out_specs=still(shape(chunk, f32)),
        scratch_shapes=[
            pltpu.VMEM((half, rows), f32),
            pltpu.VMEM((half, rows), f32),
            pltpu.VMEM((parts, 2 * lanes, rows), bf16),
            pltpu.VMEM((lanes, 128), f32),
            pltpu.VMEM((lanes, hidden), f32),
            pltpu.VMEM((hidden, hidden), f32),
            pltpu.VMEM((hidden, feats), f32),
        ],
        name="middle",
    )(*operands, features, act_one, cos_one, act_two, cos_two, weight_second, third_own)
    got = lax.all_to_all(sent, "seq", 0, 0, tiled=True)

    cut = 2 * hidden // 4
    partial = jnp.sum(got[:, 4 * lanes :, cut : 2 * cut], axis=0).reshape(1, 2, 128)
    partial = jnp.broadcast_to(partial, (parts * groups, 2, 128))
    partial = lax.all_to_all(partial, ("seq", "chan"), 0, 0, tiled=True)
    total = jnp.sum(partial.reshape(parts, groups, 2, 128), axis=1) * inv_root
    total = total.reshape(4, hidden, cut).transpose(1, 0, 2).reshape(hidden, 2 * hidden)
    grad_second = total[:, :hidden]
    grad_first = total[:, hidden : hidden + weight_first.shape[0]].T

    vocab_ids = jnp.arange(vocab_size, dtype=jnp.int32)
    before = lax.dynamic_index_in_dim(packed, jnp.maximum(seq_index - 1, 0), 0, keepdims=False)
    before = before[4 * lanes + 1, 126:].astype(jnp.int32)
    before = jnp.where(seq_index > 0, before, -1)
    window_ids = jnp.concatenate([before, tokens])
    lookup = (window_ids[:, None] == vocab_ids[None, :]).astype(bf16)
    embedded = jnp.dot(lookup, embed_table, preferred_element_type=f32)
    value_rows = (
        short_conv[0] * embedded[2:]
        + short_conv[1] * embedded[1:-1]
        + short_conv[2] * embedded[:-2]
    )
    rows_shape = shape((rows, width), bf16)
    own_vocab = vocab_size // parts
    operator_out, grad_query, grad_key, grad_embed, grad_short, grad_skip, grad_third = pl.pallas_call(
        finish_kernel,
        out_shape=(
            rows_shape,
            rows_shape,
            rows_shape,
            shape((own_vocab, width), f32),
            shape((3, width), f32),
            shape((1, width), f32),
            shape((hidden, width), f32),
        ),
        in_specs=[whole] * 4,
        out_specs=[whole] * 7,
        name="finish",
    )(got, query_branch, cotangent, value_rows)
    return (
        operator_out,
        grad_query,
        grad_key,
        grad_embed,
        grad_short,
        grad_skip.reshape(width),
        grad_first,
        grad_second,
        grad_third,
    )


def solution(mesh):
    in_specs = (
        P("seq"),
        P(None, "chan"),
        P(None, "chan"),
        P("seq", "chan"),
        P("seq", "chan"),
        P("chan"),
        P(),
        P(),
        P(None, "chan"),
        P("chan"),
        P("seq", "chan"),
    )
    out_specs = (
        P("seq", "chan"),
        P("seq", "chan"),
        P("seq", "chan"),
        P("seq", "chan"),
        P(None, "chan"),
        P("chan"),
        P(),
        P(),
        P(None, "chan"),
    )
    return jax.shard_map(
        per_device, mesh=mesh, in_specs=in_specs, out_specs=out_specs, check_vma=False
    )
```

```python
import math

import jax
import jax.numpy as jnp
import numpy as np
from jax import lax
from jax.experimental import pallas as pl
from jax.experimental.pallas import tpu as pltpu
from jax.sharding import PartitionSpec as P

BANDS = 16
STEPS = 4
VOCAB = 256

two_pi = 2.0 * math.pi
f32 = jnp.float32
bf16 = jnp.bfloat16


def halves(table):
    upper = np.asarray(np.asarray(table, np.float32), bf16)
    lower = np.asarray(np.asarray(table, np.float32) - np.asarray(upper, np.float32), bf16)
    return upper, lower


def transform_tables(parts, rows, lanes):
    length = parts * rows
    freq = 4 * np.arange(parts, dtype=np.int64) + 1
    phase = freq[:, None] * np.arange(parts, dtype=np.int64)[None, :] % (4 * parts)
    angle = two_pi * phase / (4 * parts)
    stage = np.concatenate([np.cos(angle), -np.sin(angle)], axis=0)
    turn = freq[:, None] * np.arange(rows, dtype=np.int64)[None, :] % (4 * length)
    turn = two_pi * turn / (4 * length)
    inner = np.arange(rows, dtype=np.int64)
    inner = two_pi * (inner[:, None] * inner[None, :] % rows) / rows
    inner = np.concatenate([np.cos(inner), np.sin(inner)], axis=1)
    turns = np.stack([np.cos(turn), np.sin(turn)]).astype(np.float32)
    stages = [np.repeat(table, lanes, axis=1).astype(np.float32) for table in (stage, stage.T)]
    return stages, halves(inner), turns


def feature_table(length):
    positions = np.arange(length, dtype=np.int64)
    frequency = 2 ** np.arange(BANDS, dtype=np.int64) + 1
    phases = frequency[:, None] * positions[None, :] % length
    angles = two_pi * phases / length
    table = np.concatenate([positions[None, :] / length, np.cos(angles), np.sin(angles)], axis=0)
    spare = -table.shape[0] % 8
    return np.asarray(np.pad(table, ((0, spare), (0, 0))), np.float32)


def split(block):
    upper = block.astype(bf16)
    return upper, (block - upper.astype(f32)).astype(bf16)


def dot(left, right):
    return jnp.dot(left, right, preferred_element_type=f32)


def dot_last(left, right):
    return lax.dot_general(left, right, (((1,), (1,)), ((), ())), preferred_element_type=f32)


def product(left, right, by=dot):
    return by(left[0], right[0]) + (by(left[1], right[0]) + by(left[0], right[1]))


def product_last(left, right):
    return product(left, right, dot_last)


def sine_cosine(angle):
    turns = jnp.floor(angle * (2.0 / math.pi) + 0.5)
    rest = angle - turns * 1.5703125
    rest = rest - turns * 4.837512969970703125e-4
    rest = rest - turns * 7.54978995489188216e-8
    square = rest * rest
    sine = ((-1.9515295891e-4 * square + 8.3321608736e-3) * square - 1.6666654611e-1) * square
    sine = sine * rest + rest
    cosine = (2.443315711809948e-5 * square - 1.388731625493765e-3) * square
    cosine = (cosine + 4.166664568298827e-2) * square * square - 0.5 * square + 1.0
    quarter = turns.astype(jnp.int32)
    odd = (quarter & 1) == 1
    sine, cosine = jnp.where(odd, cosine, sine), jnp.where(odd, sine, cosine)
    sine = jnp.where((quarter & 2) == 2, -sine, sine)
    cosine = jnp.where(((quarter + 1) & 2) == 2, -cosine, cosine)
    return sine, cosine


def spread_stage(table_ref, lanes):
    table = table_ref[...]
    count, width = table.shape
    wide = jnp.broadcast_to(table[:, None, :], (count, lanes, width)).reshape(count * lanes, width)
    row = lax.broadcasted_iota(jnp.int32, wide.shape, 0) & (lanes - 1)
    column = lax.broadcasted_iota(jnp.int32, wide.shape, 1) & (lanes - 1)
    return split(jnp.where(row == column, wide, 0.0))


def spread_turns(turn_ref, lanes):
    def one(table):
        parts, rows = table.shape
        wide = jnp.broadcast_to(table[:, None, :], (parts, lanes, rows))
        return wide.reshape(parts * lanes, rows)

    return one(turn_ref[0]), one(turn_ref[1])


def forward(block, first, inner, turns):
    half, rows = block.shape
    stage = product(first, split(block))
    real, imag = stage[:half], stage[half:]
    turned_real = real * turns[0] + imag * turns[1]
    turned_imag = imag * turns[0] - real * turns[1]
    along = product(split(turned_real), inner)
    across = product(split(turned_imag), inner)
    return along[:, :rows] + across[:, rows:], across[:, :rows] - along[:, rows:]


def inverse(spectrum, first_back, inner, turns, length):
    half, rows = spectrum[0].shape
    along = product(split(spectrum[0]), inner)
    across = product(split(spectrum[1]), inner)
    real = along[:, :rows] - across[:, rows:]
    imag = across[:, :rows] + along[:, rows:]
    turned_real = real * turns[0] - imag * turns[1]
    turned_imag = imag * turns[0] + real * turns[1]
    turned = jnp.concatenate([turned_real, turned_imag], axis=0)
    return product(first_back, split(turned)) * (1.0 / length)


def times(left, right):
    return left[0] * right[0] - left[1] * right[1], left[0] * right[1] + left[1] * right[0]


def against(left, right):
    return left[0] * right[0] + left[1] * right[1], left[0] * right[1] - left[1] * right[0]


def shift_back(block, lanes, steps):
    rolled = pltpu.roll(block, steps, 1)
    before = jnp.concatenate([jnp.zeros_like(rolled[:lanes]), rolled[:-lanes]], axis=0)
    column = lax.broadcasted_iota(jnp.int32, block.shape, 1)
    return jnp.where(column < steps, before, rolled)


def shift_ahead(block, lanes, steps):
    width = block.shape[1]
    rolled = pltpu.roll(block, width - steps, 1)
    after = jnp.concatenate([rolled[lanes:], jnp.zeros_like(rolled[:lanes])], axis=0)
    column = lax.broadcasted_iota(jnp.int32, block.shape, 1)
    return jnp.where(column >= width - steps, after, rolled)


def pack_kernel(key_ref, query_ref, cotangent_ref, token_ref, out_ref):
    parts = out_ref.shape[0]
    rows = key_ref.shape[0]
    lanes = key_ref.shape[1] // parts
    key_cols = key_ref[...].astype(f32).T
    grad_cols = (cotangent_ref[...].astype(f32) * query_ref[...].astype(f32)).T
    place = 0
    for block in (key_cols, grad_cols):
        for start in range(0, rows, 128):
            piece = block[:, start : start + 128].reshape(parts, lanes, 128)
            out_ref[:, place : place + lanes, :] = piece
            place += lanes
    ids = token_ref[...].astype(f32)
    ids = jnp.concatenate([ids, jnp.zeros((lanes - ids.shape[0], 128), f32)], axis=0)
    out_ref[:, place : place + lanes, :] = jnp.broadcast_to(ids[None], (parts, lanes, 128))


def front_kernel(
    feature_ref,
    first_ref,
    second_ref,
    third_ref,
    param_ref,
    stage_ref,
    in_hi,
    in_lo,
    turn_ref,
    act_one_ref,
    cos_one_ref,
    act_two_ref,
    cos_two_ref,
    window_ref,
    spec_ref,
    filter_ref,
):
    step = pl.program_id(0)
    lanes = third_ref.shape[0]
    half, rows = window_ref.shape
    length = half // lanes * rows
    block = feature_ref.shape[1]
    pre_one = product(split(first_ref[...]), split(feature_ref[...]))
    act_one, cos_one = sine_cosine(pre_one)
    act_one_ref[...] = act_one
    cos_one_ref[...] = cos_one
    pre_two = product(split(second_ref[...]), split(act_one))
    act_two, cos_two = sine_cosine(pre_two)
    act_two_ref[...] = act_two
    cos_two_ref[...] = cos_two
    shaped = product(split(third_ref[...]), split(act_two))
    count = block // rows
    for part in range(count):
        place = pl.multiple_of((step * count + part) * lanes, lanes)
        filter_ref[pl.ds(place, lanes), :] = shaped[:, part * rows : (part + 1) * rows]

    @pl.when(step == STEPS - 1)
    def _():
        row = lax.broadcasted_iota(jnp.int32, (half, rows), 0)
        column = lax.broadcasted_iota(jnp.int32, (half, rows), 1)
        position = (row // lanes * rows + column).astype(f32)
        window = param_ref[:, 1:2] * jnp.exp(-param_ref[:, 0:1] * position)
        window_ref[...] = window
        first = spread_stage(stage_ref, lanes)
        inner = (in_hi[...], in_lo[...])
        turns = spread_turns(turn_ref, lanes)
        real, imag = forward(filter_ref[...] * window, first, inner, turns)
        spec_ref[0] = real
        spec_ref[1] = imag


def received(packed_ref, place, lanes):
    parts = packed_ref.shape[0]
    pair = [
        packed_ref[:, at : at + lanes, :].reshape(parts * lanes, 128)
        for at in (place, place + lanes)
    ]
    return jnp.concatenate(pair, axis=1)


def matches(packed_ref, part, lanes, vocab):
    ids = packed_ref[part, 4 * lanes : 4 * lanes + 2, :]
    ids = jnp.concatenate([ids[0:1], ids[1:2]], axis=1)
    names = lax.broadcasted_iota(jnp.int32, (vocab, ids.shape[1]), 0).astype(f32)
    return jnp.where(names == ids, 1.0, 0.0).astype(bf16)


def lagged_values(embedded, param_ref, lanes):
    lagged = [embedded, shift_back(embedded, lanes, 1), shift_back(embedded, lanes, 2)]
    gains = [param_ref[:, 3 + lag : 4 + lag] for lag in range(3)]
    return lagged, gains, gains[0] * lagged[0] + gains[1] * lagged[1] + gains[2] * lagged[2]


def filter_kernel(
    packed_ref,
    embed_ref,
    param_ref,
    window_ref,
    stage_ref,
    back_ref,
    in_hi,
    in_lo,
    turn_ref,
    feature_ref,
    act_one_ref,
    cos_one_ref,
    act_two_ref,
    cos_two_ref,
    second_ref,
    third_ref,
    hidden_ref,
    third_acc,
    embedded_ref,
    keyed_spec_ref,
    grad_spec_ref,
    shaped_ref,
    second_acc,
    first_acc,
):
    step = pl.program_id(0)
    parts = packed_ref.shape[0]
    half, rows = window_ref.shape
    lanes = half // parts
    length = parts * rows
    vocab = embed_ref.shape[1]
    hidden = second_ref.shape[0]

    @pl.when(step == 0)
    def _():
        third_acc[...] = jnp.zeros_like(third_acc)
        second_acc[...] = jnp.zeros_like(second_acc)
        first_acc[...] = jnp.zeros_like(first_acc)
        table = embed_ref[...]

        def look_up(part, carry):
            place = pl.multiple_of(part * lanes, lanes)
            found = dot(table, matches(packed_ref, part, lanes, vocab))
            embedded_ref[pl.ds(place, lanes), :] = found
            return carry

        lax.fori_loop(0, parts, look_up, 0, unroll=4)
        key_all = received(packed_ref, 0, lanes)
        grad_z = received(packed_ref, 2 * lanes, lanes)
        _, _, value = lagged_values(embedded_ref[...], param_ref, lanes)
        first = spread_stage(stage_ref, lanes)
        first_back = spread_stage(back_ref, lanes)
        inner = (in_hi[...], in_lo[...])
        turns = spread_turns(turn_ref, lanes)
        keyed_spec = forward(key_all * value, first, inner, turns)
        grad_spec = forward(grad_z, first, inner, turns)
        for ref, spectrum in ((keyed_spec_ref, keyed_spec), (grad_spec_ref, grad_spec)):
            ref[0] = spectrum[0]
            ref[1] = spectrum[1]
        grad_filter = inverse(against(keyed_spec, grad_spec), first_back, inner, turns, length)
        shaped_ref[...] = grad_filter * window_ref[...]

    block = feature_ref.shape[1]
    count = block // rows
    pieces = []
    for part in range(count):
        place = pl.multiple_of((step * count + part) * lanes, lanes)
        pieces.append(shaped_ref[pl.ds(place, lanes), :])
    grad_shaped = split(jnp.concatenate(pieces, axis=1))
    act_two = split(act_two_ref[...])
    third_acc[...] += product_last(grad_shaped, act_two)
    grad_pre_two = product(split(third_ref[...]), grad_shaped) * cos_two_ref[...]
    grad_pre_two = split(grad_pre_two)
    second_acc[...] += product_last(split(act_one_ref[...]), grad_pre_two)
    grad_pre_one = product(split(second_ref[...]), grad_pre_two) * cos_one_ref[...]
    first_acc[...] += product_last(split(grad_pre_one), split(feature_ref[...]))

    @pl.when(step == STEPS - 1)
    def _():
        spare = jnp.zeros((hidden, hidden - first_acc.shape[1]), f32)
        joined = (second_acc[...], first_acc[...], spare)
        inv_root = 1.0 / math.sqrt(length)
        hidden_ref[...] = (jnp.concatenate(joined, axis=1) * inv_root).reshape(hidden_ref.shape)


def back_kernel(
    packed_ref,
    param_ref,
    spec_ref,
    back_ref,
    in_hi,
    in_lo,
    turn_ref,
    embedded_ref,
    keyed_spec_ref,
    grad_spec_ref,
    inner_ref,
    grad_ref,
):
    parts = packed_ref.shape[0]
    half, rows = embedded_ref.shape
    lanes = half // parts
    length = parts * rows
    key_all = received(packed_ref, 0, lanes)
    grad_z = received(packed_ref, 2 * lanes, lanes)
    _, _, value = lagged_values(embedded_ref[...], param_ref, lanes)
    first_back = spread_stage(back_ref, lanes)
    inner = (in_hi[...], in_lo[...])
    turns = spread_turns(turn_ref, lanes)
    keyed_spec = (keyed_spec_ref[0], keyed_spec_ref[1])
    grad_spec = (grad_spec_ref[0], grad_spec_ref[1])
    filter_spec = (spec_ref[0], spec_ref[1])
    back = lambda spectrum: inverse(spectrum, first_back, inner, turns, length)
    skip_gain = param_ref[:, 2:3]
    inner_ref[...] = back(times(keyed_spec, filter_spec)) + skip_gain * (key_all * value)
    grad_ref[...] = back(against(filter_spec, grad_spec)) + skip_gain * grad_z


def send_kernel(
    packed_ref, param_ref, embedded_ref, inner_ref, grad_ref, third_ref, hidden_ref, out_ref, pieces_ref
):
    parts = packed_ref.shape[0]
    half, rows = embedded_ref.shape
    lanes = half // parts
    hidden = third_ref.shape[1]
    key_all = received(packed_ref, 0, lanes)
    grad_z = received(packed_ref, 2 * lanes, lanes)
    lagged, gains, value = lagged_values(embedded_ref[...], param_ref, lanes)
    grad_keyed = grad_ref[...]
    place = 0
    for block in (inner_ref[...], grad_keyed):
        for start in range(0, rows, 128):
            piece = block[:, start : start + 128].reshape(parts, lanes, 128)
            out_ref[:, place : place + lanes, :] = piece
            place += lanes
    grad_value = grad_keyed * key_all

    def per_channel(block):
        return jnp.sum(jnp.sum(block.reshape(parts, lanes, rows), axis=0), axis=1, keepdims=True)

    tails = [per_channel(grad_value * lagged[lag]) for lag in range(3)]
    tails.append(per_channel(grad_z * (key_all * value)))
    scattered = gains[0] * grad_value
    for lag in (1, 2):
        scattered = scattered + gains[lag] * shift_ahead(grad_value, lanes, lag)
    upper, lower = split(scattered)
    both = (upper.reshape(parts, lanes, rows), lower.reshape(parts, lanes, rows))
    pieces_ref[...] = jnp.concatenate(both, axis=1)

    def collect(part, total):
        return total + dot_last(pieces_ref[part], matches(packed_ref, part, lanes, VOCAB))

    total = lax.fori_loop(0, parts, collect, jnp.zeros((2 * lanes, VOCAB), f32), unroll=4)
    embed_part = total[:lanes] + total[lanes:]
    share = VOCAB // parts
    low, high = 4 * lanes, 5 * lanes
    out_ref[:, low:high, :] = jnp.zeros((parts, lanes, 128), f32)
    for part in range(parts):
        own = embed_part[:, part * share : (part + 1) * share]
        out_ref[part, low:high, 0:share] = own
    third_part = jnp.broadcast_to(third_ref[...][None], (parts, lanes, hidden))
    out_ref[:, low:high, 128 - hidden : 128] = third_part
    for at, tail in enumerate(tails):
        out_ref[:, low:high, 16 + at : 17 + at] = jnp.broadcast_to(tail[None], (parts, lanes, 1))
    hidden_sum = jnp.sum(hidden_ref[...], axis=0)
    out_ref[:, high:, :] = jnp.broadcast_to(hidden_sum[None], (parts,) + hidden_sum.shape)


def finish_kernel(
    packed_ref,
    query_ref,
    cotangent_ref,
    value_ref,
    out_ref,
    grad_query_ref,
    grad_key_ref,
    embed_ref,
    short_ref,
    skip_ref,
    third_ref,
):
    parts = packed_ref.shape[0]
    width = query_ref.shape[1]
    rows = query_ref.shape[0]
    lanes = width // parts
    inv_root = 1.0 / math.sqrt(parts * rows)

    def crossed(place):
        tile = lambda at: packed_ref[:, at : at + lanes, :].reshape(width, 128)
        return jnp.concatenate([tile(place).T, tile(place + lanes).T], axis=0)

    inner_sum = crossed(0)
    out_ref[...] = (query_ref[...].astype(f32) * inner_sum).astype(bf16)
    grad_query_ref[...] = (cotangent_ref[...].astype(f32) * inner_sum).astype(bf16)
    grad_key_ref[...] = (crossed(2 * lanes) * value_ref[...]).astype(bf16)
    small = packed_ref[:, 4 * lanes : 5 * lanes, :].reshape(width, 128).T * inv_root
    embed_ref[...] = small[0 : embed_ref.shape[0]]
    short_ref[...] = small[16:19]
    skip_ref[...] = small[19:20]
    third_ref[...] = small[128 - third_ref.shape[0] :]


def per_device(
    tokens,
    embed_table,
    short_conv,
    query_branch,
    key_branch,
    decay_rate,
    weight_first,
    weight_second,
    weight_third,
    skip_gain,
    cotangent,
):
    parts = lax.axis_size("seq")
    groups = lax.axis_size("chan")
    seq_index = lax.axis_index("seq")
    rows, width = query_branch.shape
    lanes = width // parts
    half = parts * lanes
    length = rows * parts
    vocab_size = embed_table.shape[0]
    hidden = weight_first.shape[1]
    own = seq_index * lanes
    shape = jax.ShapeDtypeStruct
    chunk = (parts, 5 * lanes, 128)
    whole = pl.BlockSpec(memory_space=pltpu.VMEM)

    packed = pl.pallas_call(
        pack_kernel,
        out_shape=shape(chunk, f32),
        in_specs=[whole] * 4,
        out_specs=whole,
        name="pack",
    )(key_branch, query_branch, cotangent, tokens.reshape(rows // 128, 128))
    packed = lax.all_to_all(packed, "seq", 0, 0, tiled=True)

    embed_own = lax.dynamic_slice_in_dim(embed_table, own, lanes, axis=1).T
    short_own = lax.dynamic_slice_in_dim(short_conv, own, lanes, axis=1)
    decay_own = lax.dynamic_slice_in_dim(decay_rate, own, lanes, axis=0)
    skip_own = lax.dynamic_slice_in_dim(skip_gain, own, lanes, axis=0)
    third_own = lax.dynamic_slice_in_dim(weight_third, own, lanes, axis=1)
    scaling = jnp.sqrt(jnp.expm1(-2.0 * decay_own) / jnp.expm1(-2.0 * length * decay_own))
    params = [decay_own, scaling, skip_own, short_own[0], short_own[1], short_own[2]]
    params = jnp.tile(jnp.stack(params + [skip_own, skip_own], axis=1), (parts, 1))

    (stage, stage_back), (in_hi, in_lo), turns = transform_tables(parts, rows, lanes)
    features = jnp.asarray(feature_table(length))
    feats = features.shape[0]
    first_t = jnp.pad(weight_first.T, ((0, 0), (0, feats - weight_first.shape[0])))
    block = length // STEPS
    still = lambda array: pl.BlockSpec(array.shape, lambda i: (0,) * array.ndim)
    moving = lambda count: pl.BlockSpec((count, block), lambda i: (0, i))

    act = shape((hidden, length), f32)
    window_shape, spec_shape = shape((half, rows), f32), shape((2, half, rows), f32)
    second_t, third_t = weight_second.T, third_own.T
    act_one, cos_one, act_two, cos_two, window, spec = pl.pallas_call(
        front_kernel,
        out_shape=(act, act, act, act, window_shape, spec_shape),
        grid=(STEPS,),
        in_specs=[moving(feats)]
        + [still(a) for a in (first_t, second_t, third_t, params, stage, in_hi, in_lo, turns)],
        out_specs=[moving(hidden)] * 4 + [still(window_shape), still(spec_shape)],
        scratch_shapes=[pltpu.VMEM((half, rows), f32)],
        name="front",
    )(features, first_t, second_t, third_t, params, stage, in_hi, in_lo, turns)

    operands = (packed, embed_own, params, window, stage, stage_back, in_hi, in_lo, turns)
    hidden_shape = shape((groups, hidden // groups, 128), f32)
    third_shape = shape((lanes, hidden), f32)
    results = (hidden_shape, third_shape, window_shape, spec_shape, spec_shape)
    hidden_part, third_part, embedded_all, keyed_spec, grad_spec = pl.pallas_call(
        filter_kernel,
        out_shape=results,
        grid=(STEPS,),
        in_specs=[still(a) for a in operands]
        + [moving(feats)]
        + [moving(hidden)] * 4
        + [still(weight_second), still(third_own)],
        out_specs=[still(a) for a in results],
        scratch_shapes=[
            pltpu.VMEM((half, rows), f32),
            pltpu.VMEM((hidden, hidden), f32),
            pltpu.VMEM((hidden, feats), f32),
        ],
        name="filter",
    )(*operands, features, act_one, cos_one, act_two, cos_two, weight_second, third_own)

    hidden_part = lax.all_to_all(hidden_part, "chan", 0, 0, tiled=True)
    inner_sum, grad_keyed = pl.pallas_call(
        back_kernel,
        out_shape=(window_shape, window_shape),
        in_specs=[whole] * 10,
        out_specs=[whole] * 2,
        name="back",
    )(packed, params, spec, stage_back, in_hi, in_lo, turns, embedded_all, keyed_spec, grad_spec)
    sent = pl.pallas_call(
        send_kernel,
        out_shape=shape((parts, 5 * lanes + hidden // groups, 128), f32),
        in_specs=[whole] * 7,
        out_specs=whole,
        scratch_shapes=[pltpu.VMEM((parts, 2 * lanes, rows), bf16)],
        name="send",
    )(packed, params, embedded_all, inner_sum, grad_keyed, third_part, hidden_part)
    got = lax.all_to_all(sent, "seq", 0, 0, tiled=True)

    hidden_sum = jnp.sum(got[:, 5 * lanes :], axis=0)
    spread = jnp.broadcast_to(hidden_sum[None], (groups,) + hidden_sum.shape)
    total = lax.all_to_all(spread, "chan", 0, 0, tiled=True).reshape(hidden, 128)
    grad_second = total[:, :hidden]
    grad_first = total[:, hidden : hidden + weight_first.shape[0]].T

    vocab_ids = jnp.arange(vocab_size, dtype=jnp.int32)
    before = lax.dynamic_index_in_dim(packed, jnp.maximum(seq_index - 1, 0), 0, keepdims=False)
    before = before[4 * lanes + 1, 126:].astype(jnp.int32)
    before = jnp.where(seq_index > 0, before, -1)
    window_ids = jnp.concatenate([before, tokens])
    lookup = (window_ids[:, None] == vocab_ids[None, :]).astype(bf16)
    embedded = jnp.dot(lookup, embed_table, preferred_element_type=f32)
    value_rows = (
        short_conv[0] * embedded[2:]
        + short_conv[1] * embedded[1:-1]
        + short_conv[2] * embedded[:-2]
    )
    rows_shape = shape((rows, width), bf16)
    own_vocab = vocab_size // parts
    operator_out, grad_query, grad_key, grad_embed, grad_short, grad_skip, grad_third = pl.pallas_call(
        finish_kernel,
        out_shape=(
            rows_shape,
            rows_shape,
            rows_shape,
            shape((own_vocab, width), f32),
            shape((3, width), f32),
            shape((1, width), f32),
            shape((hidden, width), f32),
        ),
        in_specs=[whole] * 4,
        out_specs=[whole] * 7,
        name="finish",
    )(got, query_branch, cotangent, value_rows)
    return (
        operator_out,
        grad_query,
        grad_key,
        grad_embed,
        grad_short,
        grad_skip.reshape(width),
        grad_first,
        grad_second,
        grad_third,
    )


def solution(mesh):
    in_specs = (
        P("seq"),
        P(None, "chan"),
        P(None, "chan"),
        P("seq", "chan"),
        P("seq", "chan"),
        P("chan"),
        P(),
        P(),
        P(None, "chan"),
        P("chan"),
        P("seq", "chan"),
    )
    out_specs = (
        P("seq", "chan"),
        P("seq", "chan"),
        P("seq", "chan"),
        P("seq", "chan"),
        P(None, "chan"),
        P("chan"),
        P(),
        P(),
        P(None, "chan"),
    )
    return jax.shard_map(
        per_device, mesh=mesh, in_specs=in_specs, out_specs=out_specs, check_vma=False
    )
```

```python
import math

import jax
import jax.numpy as jnp
import numpy as np
from jax import lax
from jax.experimental import pallas as pl
from jax.experimental.pallas import tpu as pltpu
from jax.sharding import PartitionSpec as P

BANDS = 16
STEPS = 4
VOCAB = 256

two_pi = 2.0 * math.pi
f32 = jnp.float32
bf16 = jnp.bfloat16


def halves(table):
    upper = np.asarray(np.asarray(table, np.float32), bf16)
    lower = np.asarray(np.asarray(table, np.float32) - np.asarray(upper, np.float32), bf16)
    return upper, lower


def transform_tables(parts, rows, lanes):
    length = parts * rows
    freq = 4 * np.arange(parts, dtype=np.int64) + 1
    phase = freq[:, None] * np.arange(parts, dtype=np.int64)[None, :] % (4 * parts)
    angle = two_pi * phase / (4 * parts)
    stage = np.concatenate([np.cos(angle), -np.sin(angle)], axis=0)
    turn = freq[:, None] * np.arange(rows, dtype=np.int64)[None, :] % (4 * length)
    turn = two_pi * turn / (4 * length)
    inner = np.arange(rows, dtype=np.int64)
    inner = two_pi * (inner[:, None] * inner[None, :] % rows) / rows
    inner = np.concatenate([np.cos(inner), np.sin(inner)], axis=1)
    turns = np.stack([np.cos(turn), np.sin(turn)]).astype(np.float32)
    stages = [np.repeat(table, lanes, axis=1).astype(np.float32) for table in (stage, stage.T)]
    return stages, halves(inner), turns


def feature_table(length):
    positions = np.arange(length, dtype=np.int64)
    frequency = 2 ** np.arange(BANDS, dtype=np.int64) + 1
    phases = frequency[:, None] * positions[None, :] % length
    angles = two_pi * phases / length
    table = np.concatenate([positions[None, :] / length, np.cos(angles), np.sin(angles)], axis=0)
    spare = -table.shape[0] % 8
    return np.asarray(np.pad(table, ((0, spare), (0, 0))), np.float32)


def split(block):
    upper = block.astype(bf16)
    return upper, (block - upper.astype(f32)).astype(bf16)


def dot(left, right):
    return jnp.dot(left, right, preferred_element_type=f32)


def dot_last(left, right):
    return lax.dot_general(left, right, (((1,), (1,)), ((), ())), preferred_element_type=f32)


def product(left, right, by=dot):
    return by(left[0], right[0]) + (by(left[1], right[0]) + by(left[0], right[1]))


def product_last(left, right):
    return product(left, right, dot_last)


def sine_cosine(angle):
    turns = jnp.floor(angle * (2.0 / math.pi) + 0.5)
    rest = angle - turns * 1.5703125
    rest = rest - turns * 4.837512969970703125e-4
    rest = rest - turns * 7.54978995489188216e-8
    square = rest * rest
    sine = ((-1.9515295891e-4 * square + 8.3321608736e-3) * square - 1.6666654611e-1) * square
    sine = sine * rest + rest
    cosine = (2.443315711809948e-5 * square - 1.388731625493765e-3) * square
    cosine = (cosine + 4.166664568298827e-2) * square * square - 0.5 * square + 1.0
    quarter = turns.astype(jnp.int32)
    odd = (quarter & 1) == 1
    sine, cosine = jnp.where(odd, cosine, sine), jnp.where(odd, sine, cosine)
    sine = jnp.where((quarter & 2) == 2, -sine, sine)
    cosine = jnp.where(((quarter + 1) & 2) == 2, -cosine, cosine)
    return sine, cosine


def spread_stage(table_ref, lanes):
    table = table_ref[...]
    count, width = table.shape
    wide = jnp.broadcast_to(table[:, None, :], (count, lanes, width)).reshape(count * lanes, width)
    row = lax.broadcasted_iota(jnp.int32, wide.shape, 0) & (lanes - 1)
    column = lax.broadcasted_iota(jnp.int32, wide.shape, 1) & (lanes - 1)
    return split(jnp.where(row == column, wide, 0.0))


def spread_turns(turn_ref, lanes):
    def one(table):
        parts, rows = table.shape
        wide = jnp.broadcast_to(table[:, None, :], (parts, lanes, rows))
        return wide.reshape(parts * lanes, rows)

    return one(turn_ref[0]), one(turn_ref[1])


def forward(block, first, inner, turns):
    half, rows = block.shape
    stage = product(first, split(block))
    real, imag = stage[:half], stage[half:]
    turned_real = real * turns[0] + imag * turns[1]
    turned_imag = imag * turns[0] - real * turns[1]
    along = product(split(turned_real), inner)
    across = product(split(turned_imag), inner)
    return along[:, :rows] + across[:, rows:], across[:, :rows] - along[:, rows:]


def inverse(spectrum, first_back, inner, turns, length):
    half, rows = spectrum[0].shape
    along = product(split(spectrum[0]), inner)
    across = product(split(spectrum[1]), inner)
    real = along[:, :rows] - across[:, rows:]
    imag = across[:, :rows] + along[:, rows:]
    turned_real = real * turns[0] - imag * turns[1]
    turned_imag = imag * turns[0] + real * turns[1]
    turned = jnp.concatenate([turned_real, turned_imag], axis=0)
    return product(first_back, split(turned)) * (1.0 / length)


def times(left, right):
    return left[0] * right[0] - left[1] * right[1], left[0] * right[1] + left[1] * right[0]


def against(left, right):
    return left[0] * right[0] + left[1] * right[1], left[0] * right[1] - left[1] * right[0]


def shift_back(block, lanes, steps):
    rolled = pltpu.roll(block, steps, 1)
    before = jnp.concatenate([jnp.zeros_like(rolled[:lanes]), rolled[:-lanes]], axis=0)
    column = lax.broadcasted_iota(jnp.int32, block.shape, 1)
    return jnp.where(column < steps, before, rolled)


def shift_ahead(block, lanes, steps):
    width = block.shape[1]
    rolled = pltpu.roll(block, width - steps, 1)
    after = jnp.concatenate([rolled[lanes:], jnp.zeros_like(rolled[:lanes])], axis=0)
    column = lax.broadcasted_iota(jnp.int32, block.shape, 1)
    return jnp.where(column >= width - steps, after, rolled)


def pack_kernel(key_ref, query_ref, cotangent_ref, token_ref, out_ref):
    parts = out_ref.shape[0]
    rows = key_ref.shape[0]
    lanes = key_ref.shape[1] // parts
    key_cols = key_ref[...].astype(f32).T
    grad_cols = (cotangent_ref[...].astype(f32) * query_ref[...].astype(f32)).T
    place = 0
    for block in (key_cols, grad_cols):
        for start in range(0, rows, 128):
            piece = block[:, start : start + 128].reshape(parts, lanes, 128)
            out_ref[:, place : place + lanes, :] = piece
            place += lanes
    ids = token_ref[...].astype(f32)
    ids = jnp.concatenate([ids, jnp.zeros((lanes - ids.shape[0], 128), f32)], axis=0)
    out_ref[:, place : place + lanes, :] = jnp.broadcast_to(ids[None], (parts, lanes, 128))


def front_kernel(
    feature_ref,
    first_ref,
    second_ref,
    third_ref,
    param_ref,
    stage_ref,
    in_hi,
    in_lo,
    turn_ref,
    act_one_ref,
    cos_one_ref,
    act_two_ref,
    cos_two_ref,
    window_ref,
    spec_ref,
    filter_ref,
):
    step = pl.program_id(0)
    lanes = third_ref.shape[0]
    half, rows = window_ref.shape
    length = half // lanes * rows
    block = feature_ref.shape[1]
    pre_one = product(split(first_ref[...]), split(feature_ref[...]))
    act_one, cos_one = sine_cosine(pre_one)
    act_one_ref[...] = act_one
    cos_one_ref[...] = cos_one
    pre_two = product(split(second_ref[...]), split(act_one))
    act_two, cos_two = sine_cosine(pre_two)
    act_two_ref[...] = act_two
    cos_two_ref[...] = cos_two
    shaped = product(split(third_ref[...]), split(act_two))
    count = block // rows
    for part in range(count):
        place = pl.multiple_of((step * count + part) * lanes, lanes)
        filter_ref[pl.ds(place, lanes), :] = shaped[:, part * rows : (part + 1) * rows]

    @pl.when(step == STEPS - 1)
    def _():
        row = lax.broadcasted_iota(jnp.int32, (half, rows), 0)
        column = lax.broadcasted_iota(jnp.int32, (half, rows), 1)
        position = (row // lanes * rows + column).astype(f32)
        window = param_ref[:, 1:2] * jnp.exp(-param_ref[:, 0:1] * position)
        window_ref[...] = window
        first = spread_stage(stage_ref, lanes)
        inner = (in_hi[...], in_lo[...])
        turns = spread_turns(turn_ref, lanes)
        real, imag = forward(filter_ref[...] * window, first, inner, turns)
        spec_ref[0] = real
        spec_ref[1] = imag


def received(packed_ref, place, lanes):
    parts = packed_ref.shape[0]
    pair = [
        packed_ref[:, at : at + lanes, :].reshape(parts * lanes, 128)
        for at in (place, place + lanes)
    ]
    return jnp.concatenate(pair, axis=1)


def matches(packed_ref, part, lanes, vocab):
    ids = packed_ref[part, 4 * lanes : 4 * lanes + 2, :]
    ids = jnp.concatenate([ids[0:1], ids[1:2]], axis=1)
    ids = jnp.broadcast_to(ids, (16, ids.shape[1])).astype(bf16)
    names = lax.broadcasted_iota(jnp.int32, (vocab, ids.shape[1]), 0).astype(f32).astype(bf16)
    names = names.reshape(vocab // 16, 16, ids.shape[1])
    one, zero = jnp.ones((), bf16), jnp.zeros((), bf16)
    return jnp.where(names == ids[None], one, zero).reshape(vocab, ids.shape[1])


def lagged_values(embedded, param_ref, lanes):
    lagged = [embedded, shift_back(embedded, lanes, 1), shift_back(embedded, lanes, 2)]
    gains = [param_ref[:, 3 + lag : 4 + lag] for lag in range(3)]
    return lagged, gains, gains[0] * lagged[0] + gains[1] * lagged[1] + gains[2] * lagged[2]


def filter_kernel(
    packed_ref,
    embed_ref,
    param_ref,
    window_ref,
    stage_ref,
    back_ref,
    in_hi,
    in_lo,
    turn_ref,
    feature_ref,
    act_one_ref,
    cos_one_ref,
    act_two_ref,
    cos_two_ref,
    second_ref,
    third_ref,
    spec_ref,
    hidden_ref,
    third_acc,
    embedded_ref,
    inner_ref,
    grad_ref,
    shaped_ref,
    second_acc,
    first_acc,
):
    step = pl.program_id(0)
    parts = packed_ref.shape[0]
    half, rows = window_ref.shape
    lanes = half // parts
    length = parts * rows
    vocab = embed_ref.shape[1]
    hidden = second_ref.shape[0]

    @pl.when(step == 0)
    def _():
        third_acc[...] = jnp.zeros_like(third_acc)
        second_acc[...] = jnp.zeros_like(second_acc)
        first_acc[...] = jnp.zeros_like(first_acc)
        table = embed_ref[...]

        def look_up(part, carry):
            place = pl.multiple_of(part * lanes, lanes)
            found = dot(table, matches(packed_ref, part, lanes, vocab))
            embedded_ref[pl.ds(place, lanes), :] = found
            return carry

        lax.fori_loop(0, parts, look_up, 0, unroll=4)
        key_all = received(packed_ref, 0, lanes)
        grad_z = received(packed_ref, 2 * lanes, lanes)
        _, _, value = lagged_values(embedded_ref[...], param_ref, lanes)
        keyed = key_all * value
        first = spread_stage(stage_ref, lanes)
        first_back = spread_stage(back_ref, lanes)
        inner = (in_hi[...], in_lo[...])
        turns = spread_turns(turn_ref, lanes)
        keyed_spec = forward(keyed, first, inner, turns)
        grad_spec = forward(grad_z, first, inner, turns)
        back = lambda spectrum: inverse(spectrum, first_back, inner, turns, length)
        shaped_ref[...] = back(against(keyed_spec, grad_spec)) * window_ref[...]
        filter_spec = (spec_ref[0], spec_ref[1])
        skip_gain = param_ref[:, 2:3]
        inner_ref[...] = back(times(keyed_spec, filter_spec)) + skip_gain * keyed
        grad_ref[...] = back(against(filter_spec, grad_spec)) + skip_gain * grad_z

    block = feature_ref.shape[1]
    count = block // rows
    pieces = []
    for part in range(count):
        place = pl.multiple_of((step * count + part) * lanes, lanes)
        pieces.append(shaped_ref[pl.ds(place, lanes), :])
    grad_shaped = split(jnp.concatenate(pieces, axis=1))
    act_two = split(act_two_ref[...])
    third_acc[...] += product_last(grad_shaped, act_two)
    grad_pre_two = product(split(third_ref[...]), grad_shaped) * cos_two_ref[...]
    grad_pre_two = split(grad_pre_two)
    second_acc[...] += product_last(split(act_one_ref[...]), grad_pre_two)
    grad_pre_one = product(split(second_ref[...]), grad_pre_two) * cos_one_ref[...]
    first_acc[...] += product_last(split(grad_pre_one), split(feature_ref[...]))

    @pl.when(step == STEPS - 1)
    def _():
        spare = jnp.zeros((hidden, hidden - first_acc.shape[1]), f32)
        joined = (second_acc[...], first_acc[...], spare)
        inv_root = 1.0 / math.sqrt(length)
        hidden_ref[...] = (jnp.concatenate(joined, axis=1) * inv_root).reshape(hidden_ref.shape)


def send_kernel(
    packed_ref, param_ref, embedded_ref, inner_ref, grad_ref, third_ref, out_ref, pieces_ref
):
    parts = packed_ref.shape[0]
    half, rows = embedded_ref.shape
    lanes = half // parts
    hidden = third_ref.shape[1]
    key_all = received(packed_ref, 0, lanes)
    grad_z = received(packed_ref, 2 * lanes, lanes)
    lagged, gains, value = lagged_values(embedded_ref[...], param_ref, lanes)
    grad_keyed = grad_ref[...]
    place = 0
    for block in (inner_ref[...], grad_keyed):
        for start in range(0, rows, 128):
            piece = block[:, start : start + 128].reshape(parts, lanes, 128)
            out_ref[:, place : place + lanes, :] = piece
            place += lanes
    grad_value = grad_keyed * key_all

    def per_channel(block):
        return jnp.sum(jnp.sum(block.reshape(parts, lanes, rows), axis=0), axis=1, keepdims=True)

    tails = [per_channel(grad_value * lagged[lag]) for lag in range(3)]
    tails.append(per_channel(grad_z * (key_all * value)))
    scattered = gains[0] * grad_value
    for lag in (1, 2):
        scattered = scattered + gains[lag] * shift_ahead(grad_value, lanes, lag)
    upper, lower = split(scattered)
    both = (upper.reshape(parts, lanes, rows), lower.reshape(parts, lanes, rows))
    pieces_ref[...] = jnp.concatenate(both, axis=1)

    def collect(part, total):
        return total + dot_last(pieces_ref[part], matches(packed_ref, part, lanes, VOCAB))

    total = lax.fori_loop(0, parts, collect, jnp.zeros((2 * lanes, VOCAB), f32), unroll=4)
    embed_part = total[:lanes] + total[lanes:]
    share = VOCAB // parts
    low, high = 4 * lanes, 5 * lanes
    out_ref[:, low:high, :] = jnp.zeros((parts, lanes, 128), f32)
    for part in range(parts):
        own = embed_part[:, part * share : (part + 1) * share]
        out_ref[part, low:high, 0:share] = own
    third_part = jnp.broadcast_to(third_ref[...][None], (parts, lanes, hidden))
    out_ref[:, low:high, 128 - hidden : 128] = third_part
    for at, tail in enumerate(tails):
        out_ref[:, low:high, 16 + at : 17 + at] = jnp.broadcast_to(tail[None], (parts, lanes, 1))


def finish_kernel(
    packed_ref,
    query_ref,
    cotangent_ref,
    value_ref,
    out_ref,
    grad_query_ref,
    grad_key_ref,
    embed_ref,
    short_ref,
    skip_ref,
    third_ref,
):
    parts = packed_ref.shape[0]
    width = query_ref.shape[1]
    rows = query_ref.shape[0]
    lanes = width // parts
    inv_root = 1.0 / math.sqrt(parts * rows)

    def crossed(place):
        tile = lambda at: packed_ref[:, at : at + lanes, :].reshape(width, 128)
        return jnp.concatenate([tile(place).T, tile(place + lanes).T], axis=0)

    inner_sum = crossed(0)
    out_ref[...] = (query_ref[...].astype(f32) * inner_sum).astype(bf16)
    grad_query_ref[...] = (cotangent_ref[...].astype(f32) * inner_sum).astype(bf16)
    grad_key_ref[...] = (crossed(2 * lanes) * value_ref[...]).astype(bf16)
    small = packed_ref[:, 4 * lanes : 5 * lanes, :].reshape(width, 128).T * inv_root
    embed_ref[...] = small[0 : embed_ref.shape[0]]
    short_ref[...] = small[16:19]
    skip_ref[...] = small[19:20]
    third_ref[...] = small[128 - third_ref.shape[0] :]


def per_device(
    tokens,
    embed_table,
    short_conv,
    query_branch,
    key_branch,
    decay_rate,
    weight_first,
    weight_second,
    weight_third,
    skip_gain,
    cotangent,
):
    parts = lax.axis_size("seq")
    groups = lax.axis_size("chan")
    seq_index = lax.axis_index("seq")
    rows, width = query_branch.shape
    lanes = width // parts
    half = parts * lanes
    length = rows * parts
    vocab_size = embed_table.shape[0]
    hidden = weight_first.shape[1]
    own = seq_index * lanes
    shape = jax.ShapeDtypeStruct
    chunk = (parts, 5 * lanes, 128)
    whole = pl.BlockSpec(memory_space=pltpu.VMEM)

    packed = pl.pallas_call(
        pack_kernel,
        out_shape=shape(chunk, f32),
        in_specs=[whole] * 4,
        out_specs=whole,
        name="pack",
    )(key_branch, query_branch, cotangent, tokens.reshape(rows // 128, 128))
    packed = lax.all_to_all(packed, "seq", 0, 0, tiled=True)

    embed_own = lax.dynamic_slice_in_dim(embed_table, own, lanes, axis=1).T
    short_own = lax.dynamic_slice_in_dim(short_conv, own, lanes, axis=1)
    decay_own = lax.dynamic_slice_in_dim(decay_rate, own, lanes, axis=0)
    skip_own = lax.dynamic_slice_in_dim(skip_gain, own, lanes, axis=0)
    third_own = lax.dynamic_slice_in_dim(weight_third, own, lanes, axis=1)
    scaling = jnp.sqrt(jnp.expm1(-2.0 * decay_own) / jnp.expm1(-2.0 * length * decay_own))
    params = [decay_own, scaling, skip_own, short_own[0], short_own[1], short_own[2]]
    params = jnp.tile(jnp.stack(params + [skip_own, skip_own], axis=1), (parts, 1))

    (stage, stage_back), (in_hi, in_lo), turns = transform_tables(parts, rows, lanes)
    features = jnp.asarray(feature_table(length))
    feats = features.shape[0]
    first_t = jnp.pad(weight_first.T, ((0, 0), (0, feats - weight_first.shape[0])))
    block = length // STEPS
    still = lambda array: pl.BlockSpec(array.shape, lambda i: (0,) * array.ndim)
    moving = lambda count: pl.BlockSpec((count, block), lambda i: (0, i))

    act = shape((hidden, length), f32)
    window_shape, spec_shape = shape((half, rows), f32), shape((2, half, rows), f32)
    second_t, third_t = weight_second.T, third_own.T
    act_one, cos_one, act_two, cos_two, window, spec = pl.pallas_call(
        front_kernel,
        out_shape=(act, act, act, act, window_shape, spec_shape),
        grid=(STEPS,),
        in_specs=[moving(feats)]
        + [still(a) for a in (first_t, second_t, third_t, params, stage, in_hi, in_lo, turns)],
        out_specs=[moving(hidden)] * 4 + [still(window_shape), still(spec_shape)],
        scratch_shapes=[pltpu.VMEM((half, rows), f32)],
        name="front",
    )(features, first_t, second_t, third_t, params, stage, in_hi, in_lo, turns)

    operands = (packed, embed_own, params, window, stage, stage_back, in_hi, in_lo, turns)
    hidden_shape = shape((groups, hidden // groups, 128), f32)
    third_shape = shape((lanes, hidden), f32)
    results = (hidden_shape, third_shape) + (window_shape,) * 3
    hidden_part, third_part, embedded_all, inner_sum, grad_keyed = pl.pallas_call(
        filter_kernel,
        out_shape=results,
        grid=(STEPS,),
        in_specs=[still(a) for a in operands]
        + [moving(feats)]
        + [moving(hidden)] * 4
        + [still(weight_second), still(third_own), still(spec)],
        out_specs=[still(a) for a in results],
        scratch_shapes=[
            pltpu.VMEM((half, rows), f32),
            pltpu.VMEM((hidden, hidden), f32),
            pltpu.VMEM((hidden, feats), f32),
        ],
        name="filter",
    )(*operands, features, act_one, cos_one, act_two, cos_two, weight_second, third_own, spec)

    hidden_part = lax.all_to_all(hidden_part, "chan", 0, 0, tiled=True)
    sent = pl.pallas_call(
        send_kernel,
        out_shape=shape((parts, 5 * lanes + hidden // groups, 128), f32),
        in_specs=[whole] * 6,
        out_specs=whole,
        scratch_shapes=[pltpu.VMEM((parts, 2 * lanes, rows), bf16)],
        name="send",
    )(packed, params, embedded_all, inner_sum, grad_keyed, third_part)
    hidden_sum = jnp.sum(hidden_part, axis=0)
    spread = jnp.broadcast_to(hidden_sum[None], (parts,) + hidden_sum.shape)
    sent = lax.dynamic_update_slice(sent, spread, (0, 5 * lanes, 0))

    vocab_ids = jnp.arange(vocab_size, dtype=jnp.int32)
    before = lax.dynamic_index_in_dim(packed, jnp.maximum(seq_index - 1, 0), 0, keepdims=False)
    before = before[4 * lanes + 1, 126:].astype(jnp.int32)
    before = jnp.where(seq_index > 0, before, -1)
    window_ids = jnp.concatenate([before, tokens])
    lookup = (window_ids[:, None] == vocab_ids[None, :]).astype(bf16)
    embedded = jnp.dot(lookup, embed_table, preferred_element_type=f32)
    value_rows = (
        short_conv[0] * embedded[2:]
        + short_conv[1] * embedded[1:-1]
        + short_conv[2] * embedded[:-2]
    )
    sent, value_rows = lax.optimization_barrier((sent, value_rows))
    got = lax.all_to_all(sent, "seq", 0, 0, tiled=True)

    hidden_sum = jnp.sum(got[:, 5 * lanes :], axis=0)
    spread = jnp.broadcast_to(hidden_sum[None], (groups,) + hidden_sum.shape)
    total = lax.all_to_all(spread, "chan", 0, 0, tiled=True).reshape(hidden, 128)
    grad_second = total[:, :hidden]
    grad_first = total[:, hidden : hidden + weight_first.shape[0]].T

    rows_shape = shape((rows, width), bf16)
    own_vocab = vocab_size // parts
    operator_out, grad_query, grad_key, grad_embed, grad_short, grad_skip, grad_third = pl.pallas_call(
        finish_kernel,
        out_shape=(
            rows_shape,
            rows_shape,
            rows_shape,
            shape((own_vocab, width), f32),
            shape((3, width), f32),
            shape((1, width), f32),
            shape((hidden, width), f32),
        ),
        in_specs=[whole] * 4,
        out_specs=[whole] * 7,
        name="finish",
    )(got, query_branch, cotangent, value_rows)
    return (
        operator_out,
        grad_query,
        grad_key,
        grad_embed,
        grad_short,
        grad_skip.reshape(width),
        grad_first,
        grad_second,
        grad_third,
    )


def solution(mesh):
    in_specs = (
        P("seq"),
        P(None, "chan"),
        P(None, "chan"),
        P("seq", "chan"),
        P("seq", "chan"),
        P("chan"),
        P(),
        P(),
        P(None, "chan"),
        P("chan"),
        P("seq", "chan"),
    )
    out_specs = (
        P("seq", "chan"),
        P("seq", "chan"),
        P("seq", "chan"),
        P("seq", "chan"),
        P(None, "chan"),
        P("chan"),
        P(),
        P(),
        P(None, "chan"),
    )
    return jax.shard_map(
        per_device, mesh=mesh, in_specs=in_specs, out_specs=out_specs, check_vma=False
    )
```

```python
import math

import jax
import jax.numpy as jnp
import numpy as np
from jax import lax
from jax.experimental import pallas as pl
from jax.experimental.pallas import tpu as pltpu
from jax.sharding import PartitionSpec as P

BANDS = 16
STEPS = 4
VOCAB = 256

two_pi = 2.0 * math.pi
f32 = jnp.float32
bf16 = jnp.bfloat16


def halves(table):
    upper = np.asarray(np.asarray(table, np.float32), bf16)
    lower = np.asarray(np.asarray(table, np.float32) - np.asarray(upper, np.float32), bf16)
    return upper, lower


def transform_tables(parts, rows, lanes):
    length = parts * rows
    freq = 4 * np.arange(parts, dtype=np.int64) + 1
    phase = freq[:, None] * np.arange(parts, dtype=np.int64)[None, :] % (4 * parts)
    angle = two_pi * phase / (4 * parts)
    stage = np.concatenate([np.cos(angle), -np.sin(angle)], axis=0)
    turn = freq[:, None] * np.arange(rows, dtype=np.int64)[None, :] % (4 * length)
    turn = two_pi * turn / (4 * length)
    inner = np.arange(rows, dtype=np.int64)
    inner = two_pi * (inner[:, None] * inner[None, :] % rows) / rows
    inner = np.concatenate([np.cos(inner), np.sin(inner)], axis=1)
    turns = np.stack([np.cos(turn), np.sin(turn)]).astype(np.float32)
    stages = [np.repeat(table, lanes, axis=1).astype(np.float32) for table in (stage, stage.T)]
    return stages, halves(inner), turns


def feature_table(length):
    positions = np.arange(length, dtype=np.int64)
    frequency = 2 ** np.arange(BANDS, dtype=np.int64) + 1
    phases = frequency[:, None] * positions[None, :] % length
    angles = two_pi * phases / length
    table = np.concatenate([positions[None, :] / length, np.cos(angles), np.sin(angles)], axis=0)
    spare = -table.shape[0] % 16
    return np.asarray(np.pad(table, ((0, spare), (0, 0))), np.float32)


def split(block):
    upper = block.astype(bf16)
    return upper, (block - upper.astype(f32)).astype(bf16)


def dot(left, right):
    return jnp.dot(left, right, preferred_element_type=f32)


def dot_last(left, right):
    return lax.dot_general(left, right, (((1,), (1,)), ((), ())), preferred_element_type=f32)


def product(left, right, by=dot):
    return by(left[0], right[0]) + (by(left[1], right[0]) + by(left[0], right[1]))


def product_last(left, right):
    return product(left, right, dot_last)


def deep(pair):
    return jnp.concatenate([pair[0], pair[0], pair[1]], axis=0)


def wide(matrix):
    upper = lax.reduce_precision(matrix, 8, 7)
    return jnp.concatenate([upper, matrix - upper, upper], axis=1).astype(bf16)


def sine_cosine(angle):
    turns = jnp.floor(angle * (2.0 / math.pi) + 0.5)
    rest = angle - turns * 1.5703125
    rest = rest - turns * 4.837512969970703125e-4
    rest = rest - turns * 7.54978995489188216e-8
    square = rest * rest
    sine = ((-1.9515295891e-4 * square + 8.3321608736e-3) * square - 1.6666654611e-1) * square
    sine = sine * rest + rest
    cosine = (2.443315711809948e-5 * square - 1.388731625493765e-3) * square
    cosine = (cosine + 4.166664568298827e-2) * square * square - 0.5 * square + 1.0
    quarter = turns.astype(jnp.int32)
    odd = (quarter & 1) == 1
    sine, cosine = jnp.where(odd, cosine, sine), jnp.where(odd, sine, cosine)
    sine = jnp.where((quarter & 2) == 2, -sine, sine)
    cosine = jnp.where(((quarter + 1) & 2) == 2, -cosine, cosine)
    return sine, cosine


def spread_stage(table_ref, lanes):
    table = table_ref[...]
    count, width = table.shape
    wide = jnp.broadcast_to(table[:, None, :], (count, lanes, width)).reshape(count * lanes, width)
    row = lax.broadcasted_iota(jnp.int32, wide.shape, 0) & (lanes - 1)
    column = lax.broadcasted_iota(jnp.int32, wide.shape, 1) & (lanes - 1)
    return split(jnp.where(row == column, wide, 0.0))


def spread_turns(turn_ref, lanes):
    def one(table):
        parts, rows = table.shape
        wide = jnp.broadcast_to(table[:, None, :], (parts, lanes, rows))
        return wide.reshape(parts * lanes, rows)

    return one(turn_ref[0]), one(turn_ref[1])


def forward(block, first, inner, turns):
    half, rows = block.shape
    stage = product(first, split(block))
    real, imag = stage[:half], stage[half:]
    turned_real = real * turns[0] + imag * turns[1]
    turned_imag = imag * turns[0] - real * turns[1]
    along = product(split(turned_real), inner)
    across = product(split(turned_imag), inner)
    return along[:, :rows] + across[:, rows:], across[:, :rows] - along[:, rows:]


def inverse(spectrum, first_back, inner, turns, length):
    half, rows = spectrum[0].shape
    along = product(split(spectrum[0]), inner)
    across = product(split(spectrum[1]), inner)
    real = along[:, :rows] - across[:, rows:]
    imag = across[:, :rows] + along[:, rows:]
    turned_real = real * turns[0] - imag * turns[1]
    turned_imag = imag * turns[0] + real * turns[1]
    turned = jnp.concatenate([turned_real, turned_imag], axis=0)
    return product(first_back, split(turned)) * (1.0 / length)


def times(left, right):
    return left[0] * right[0] - left[1] * right[1], left[0] * right[1] + left[1] * right[0]


def against(left, right):
    return left[0] * right[0] + left[1] * right[1], left[0] * right[1] - left[1] * right[0]


def shift_back(block, lanes, steps):
    rolled = pltpu.roll(block, steps, 1)
    before = jnp.concatenate([jnp.zeros_like(rolled[:lanes]), rolled[:-lanes]], axis=0)
    column = lax.broadcasted_iota(jnp.int32, block.shape, 1)
    return jnp.where(column < steps, before, rolled)


def shift_ahead(block, lanes, steps):
    width = block.shape[1]
    rolled = pltpu.roll(block, width - steps, 1)
    after = jnp.concatenate([rolled[lanes:], jnp.zeros_like(rolled[:lanes])], axis=0)
    column = lax.broadcasted_iota(jnp.int32, block.shape, 1)
    return jnp.where(column >= width - steps, after, rolled)


def pack_kernel(key_ref, query_ref, cotangent_ref, token_ref, out_ref):
    parts = out_ref.shape[0]
    rows = key_ref.shape[0]
    lanes = key_ref.shape[1] // parts
    key_cols = key_ref[...].astype(f32).T
    grad_cols = (cotangent_ref[...].astype(f32) * query_ref[...].astype(f32)).T
    place = 0
    for block in (key_cols, grad_cols):
        for start in range(0, rows, 128):
            piece = block[:, start : start + 128].reshape(parts, lanes, 128)
            out_ref[:, place : place + lanes, :] = piece
            place += lanes
    ids = token_ref[...].astype(f32)
    ids = jnp.concatenate([ids, jnp.zeros((lanes - ids.shape[0], 128), f32)], axis=0)
    out_ref[:, place : place + lanes, :] = jnp.broadcast_to(ids[None], (parts, lanes, 128))


def front_kernel(
    feature_ref,
    first_ref,
    second_ref,
    third_ref,
    param_ref,
    stage_ref,
    in_hi,
    in_lo,
    turn_ref,
    upper_ref,
    lower_ref,
    cos_one_ref,
    cos_two_ref,
    window_ref,
    spec_ref,
    filter_ref,
):
    step = pl.program_id(0)
    lanes = third_ref.shape[0]
    half, rows = window_ref.shape
    length = half // lanes * rows
    block = feature_ref.shape[1]
    feature = split(feature_ref[...])
    act_one, cos_one = sine_cosine(dot(first_ref[...], deep(feature)))
    cos_one_ref[...] = cos_one
    act_one = split(act_one)
    act_two, cos_two = sine_cosine(dot(second_ref[...], deep(act_one)))
    cos_two_ref[...] = cos_two
    act_two = split(act_two)
    shaped = dot(third_ref[...], deep(act_two))
    for ref, half_of in ((upper_ref, 0), (lower_ref, 1)):
        both = (act_two[half_of], act_one[half_of], feature[half_of])
        ref[...] = jnp.concatenate(both, axis=0)
    count = block // rows
    for part in range(count):
        place = pl.multiple_of((step * count + part) * lanes, lanes)
        filter_ref[pl.ds(place, lanes), :] = shaped[:, part * rows : (part + 1) * rows]

    @pl.when(step == STEPS - 1)
    def _():
        row = lax.broadcasted_iota(jnp.int32, (half, rows), 0)
        column = lax.broadcasted_iota(jnp.int32, (half, rows), 1)
        position = (row // lanes * rows + column).astype(f32)
        window = param_ref[:, 1:2] * jnp.exp(-param_ref[:, 0:1] * position)
        window_ref[...] = window
        first = spread_stage(stage_ref, lanes)
        inner = (in_hi[...], in_lo[...])
        turns = spread_turns(turn_ref, lanes)
        real, imag = forward(filter_ref[...] * window, first, inner, turns)
        spec_ref[0] = real
        spec_ref[1] = imag


def received(packed_ref, place, lanes):
    parts = packed_ref.shape[0]
    pair = [
        packed_ref[:, at : at + lanes, :].reshape(parts * lanes, 128)
        for at in (place, place + lanes)
    ]
    return jnp.concatenate(pair, axis=1)


def matches(packed_ref, part, lanes, vocab):
    ids = packed_ref[part, 4 * lanes : 4 * lanes + 2, :]
    ids = jnp.concatenate([ids[0:1], ids[1:2]], axis=1)
    ids = jnp.broadcast_to(ids, (16, ids.shape[1])).astype(bf16)
    names = lax.broadcasted_iota(jnp.int32, (vocab, ids.shape[1]), 0).astype(f32).astype(bf16)
    names = names.reshape(vocab // 16, 16, ids.shape[1])
    one, zero = jnp.ones((), bf16), jnp.zeros((), bf16)
    return jnp.where(names == ids[None], one, zero).reshape(vocab, ids.shape[1])


def lagged_values(embedded, param_ref, lanes):
    lagged = [embedded, shift_back(embedded, lanes, 1), shift_back(embedded, lanes, 2)]
    gains = [param_ref[:, 3 + lag : 4 + lag] for lag in range(3)]
    return lagged, gains, gains[0] * lagged[0] + gains[1] * lagged[1] + gains[2] * lagged[2]


def filter_kernel(
    packed_ref,
    embed_ref,
    param_ref,
    window_ref,
    stage_ref,
    back_ref,
    in_hi,
    in_lo,
    turn_ref,
    upper_ref,
    lower_ref,
    cos_one_ref,
    cos_two_ref,
    second_ref,
    third_ref,
    spec_ref,
    hidden_ref,
    third_part_ref,
    embedded_ref,
    inner_ref,
    grad_ref,
    shaped_ref,
    acc_ref,
):
    step = pl.program_id(0)
    parts = packed_ref.shape[0]
    half, rows = window_ref.shape
    lanes = half // parts
    length = parts * rows
    vocab = embed_ref.shape[1]
    hidden = second_ref.shape[0]

    @pl.when(step == 0)
    def _():
        acc_ref[...] = jnp.zeros_like(acc_ref)
        table = embed_ref[...]

        def look_up(part, carry):
            place = pl.multiple_of(part * lanes, lanes)
            found = dot(table, matches(packed_ref, part, lanes, vocab))
            embedded_ref[pl.ds(place, lanes), :] = found
            return carry

        lax.fori_loop(0, parts, look_up, 0, unroll=4)
        key_all = received(packed_ref, 0, lanes)
        grad_z = received(packed_ref, 2 * lanes, lanes)
        _, _, value = lagged_values(embedded_ref[...], param_ref, lanes)
        keyed = key_all * value
        first = spread_stage(stage_ref, lanes)
        first_back = spread_stage(back_ref, lanes)
        inner = (in_hi[...], in_lo[...])
        turns = spread_turns(turn_ref, lanes)
        keyed_spec = forward(keyed, first, inner, turns)
        grad_spec = forward(grad_z, first, inner, turns)
        back = lambda spectrum: inverse(spectrum, first_back, inner, turns, length)
        shaped_ref[...] = back(against(keyed_spec, grad_spec)) * window_ref[...]
        filter_spec = (spec_ref[0], spec_ref[1])
        skip_gain = param_ref[:, 2:3]
        inner_ref[...] = back(times(keyed_spec, filter_spec)) + skip_gain * keyed
        grad_ref[...] = back(against(filter_spec, grad_spec)) + skip_gain * grad_z

    block = upper_ref.shape[1]
    count = block // rows
    pieces = []
    for part in range(count):
        place = pl.multiple_of((step * count + part) * lanes, lanes)
        pieces.append(shaped_ref[pl.ds(place, lanes), :])
    grad_shaped = jnp.concatenate(pieces, axis=1)
    grad_shaped = split(jnp.concatenate([grad_shaped, jnp.zeros_like(grad_shaped)], axis=0))
    grad_pre_two = split(dot(third_ref[...], deep(grad_shaped)) * cos_two_ref[...])
    grad_pre_one = split(dot(second_ref[...], deep(grad_pre_two)) * cos_one_ref[...])
    left = [
        jnp.concatenate([grad_shaped[i], grad_pre_two[i], grad_pre_one[i]], axis=0) for i in range(2)
    ]
    count = left[0].shape[0]
    both = dot_last(jnp.concatenate(left, axis=0), upper_ref[...])
    acc_ref[...] += both[:count] + both[count:] + dot_last(left[0], lower_ref[...])

    @pl.when(step == STEPS - 1)
    def _():
        inv_root = 1.0 / math.sqrt(length)
        two, one = 2 * lanes, 2 * lanes + hidden
        third_part_ref[...] = acc_ref[0:lanes, 0:hidden]
        second_part = acc_ref[two:one, hidden : 2 * hidden]
        first_part = acc_ref[one:, 2 * hidden :]
        spare = jnp.zeros((hidden, hidden - first_part.shape[1]), f32)
        joined = jnp.concatenate([second_part, first_part, spare], axis=1) * inv_root
        hidden_ref[...] = joined.reshape(hidden_ref.shape)


def send_kernel(
    packed_ref, param_ref, embedded_ref, inner_ref, grad_ref, third_ref, out_ref, pieces_ref
):
    parts = packed_ref.shape[0]
    half, rows = embedded_ref.shape
    lanes = half // parts
    hidden = third_ref.shape[1]
    key_all = received(packed_ref, 0, lanes)
    grad_z = received(packed_ref, 2 * lanes, lanes)
    lagged, gains, value = lagged_values(embedded_ref[...], param_ref, lanes)
    grad_keyed = grad_ref[...]
    place = 0
    for block in (inner_ref[...], grad_keyed):
        for start in range(0, rows, 128):
            piece = block[:, start : start + 128].reshape(parts, lanes, 128)
            out_ref[:, place : place + lanes, :] = piece
            place += lanes
    grad_value = grad_keyed * key_all

    def per_channel(block):
        return jnp.sum(jnp.sum(block.reshape(parts, lanes, rows), axis=0), axis=1, keepdims=True)

    tails = [per_channel(grad_value * lagged[lag]) for lag in range(3)]
    tails.append(per_channel(grad_z * (key_all * value)))
    scattered = gains[0] * grad_value
    for lag in (1, 2):
        scattered = scattered + gains[lag] * shift_ahead(grad_value, lanes, lag)
    upper, lower = split(scattered)
    both = (upper.reshape(parts, lanes, rows), lower.reshape(parts, lanes, rows))
    pieces_ref[...] = jnp.concatenate(both, axis=1)

    def collect(part, total):
        return total + dot_last(pieces_ref[part], matches(packed_ref, part, lanes, VOCAB))

    total = lax.fori_loop(0, parts, collect, jnp.zeros((2 * lanes, VOCAB), f32), unroll=4)
    embed_part = total[:lanes] + total[lanes:]
    share = VOCAB // parts
    low, high = 4 * lanes, 5 * lanes
    out_ref[:, low:high, :] = jnp.zeros((parts, lanes, 128), f32)
    for part in range(parts):
        own = embed_part[:, part * share : (part + 1) * share]
        out_ref[part, low:high, 0:share] = own
    third_part = jnp.broadcast_to(third_ref[...][None], (parts, lanes, hidden))
    out_ref[:, low:high, 128 - hidden : 128] = third_part
    for at, tail in enumerate(tails):
        out_ref[:, low:high, 16 + at : 17 + at] = jnp.broadcast_to(tail[None], (parts, lanes, 1))


def finish_kernel(
    packed_ref,
    query_ref,
    cotangent_ref,
    value_ref,
    out_ref,
    grad_query_ref,
    grad_key_ref,
    embed_ref,
    short_ref,
    skip_ref,
    third_ref,
):
    parts = packed_ref.shape[0]
    width = query_ref.shape[1]
    rows = query_ref.shape[0]
    lanes = width // parts
    inv_root = 1.0 / math.sqrt(parts * rows)

    def crossed(place):
        tile = lambda at: packed_ref[:, at : at + lanes, :].reshape(width, 128)
        return jnp.concatenate([tile(place).T, tile(place + lanes).T], axis=0)

    inner_sum = crossed(0)
    out_ref[...] = (query_ref[...].astype(f32) * inner_sum).astype(bf16)
    grad_query_ref[...] = (cotangent_ref[...].astype(f32) * inner_sum).astype(bf16)
    grad_key_ref[...] = (crossed(2 * lanes) * value_ref[...]).astype(bf16)
    small = packed_ref[:, 4 * lanes : 5 * lanes, :].reshape(width, 128).T * inv_root
    embed_ref[...] = small[0 : embed_ref.shape[0]]
    short_ref[...] = small[16:19]
    skip_ref[...] = small[19:20]
    third_ref[...] = small[128 - third_ref.shape[0] :]


def per_device(
    tokens,
    embed_table,
    short_conv,
    query_branch,
    key_branch,
    decay_rate,
    weight_first,
    weight_second,
    weight_third,
    skip_gain,
    cotangent,
):
    parts = lax.axis_size("seq")
    groups = lax.axis_size("chan")
    seq_index = lax.axis_index("seq")
    rows, width = query_branch.shape
    lanes = width // parts
    half = parts * lanes
    length = rows * parts
    vocab_size = embed_table.shape[0]
    hidden = weight_first.shape[1]
    own = seq_index * lanes
    shape = jax.ShapeDtypeStruct
    chunk = (parts, 5 * lanes, 128)
    whole = pl.BlockSpec(memory_space=pltpu.VMEM)

    packed = pl.pallas_call(
        pack_kernel,
        out_shape=shape(chunk, f32),
        in_specs=[whole] * 4,
        out_specs=whole,
        name="pack",
    )(key_branch, query_branch, cotangent, tokens.reshape(rows // 128, 128))
    packed = lax.all_to_all(packed, "seq", 0, 0, tiled=True)

    embed_own = lax.dynamic_slice_in_dim(embed_table, own, lanes, axis=1).T
    short_own = lax.dynamic_slice_in_dim(short_conv, own, lanes, axis=1)
    decay_own = lax.dynamic_slice_in_dim(decay_rate, own, lanes, axis=0)
    skip_own = lax.dynamic_slice_in_dim(skip_gain, own, lanes, axis=0)
    third_own = lax.dynamic_slice_in_dim(weight_third, own, lanes, axis=1)
    scaling = jnp.sqrt(jnp.expm1(-2.0 * decay_own) / jnp.expm1(-2.0 * length * decay_own))
    params = [decay_own, scaling, skip_own, short_own[0], short_own[1], short_own[2]]
    params = jnp.tile(jnp.stack(params + [skip_own, skip_own], axis=1), (parts, 1))

    (stage, stage_back), (in_hi, in_lo), turns = transform_tables(parts, rows, lanes)
    features = jnp.asarray(feature_table(length))
    feats = features.shape[0]
    first_t = jnp.pad(weight_first.T, ((0, 0), (0, feats - weight_first.shape[0])))
    block = length // STEPS
    still = lambda array: pl.BlockSpec(array.shape, lambda i: (0,) * array.ndim)
    moving = lambda count: pl.BlockSpec((count, block), lambda i: (0, i))

    act, joint = shape((hidden, length), f32), shape((2 * hidden + feats, length), bf16)
    window_shape, spec_shape = shape((half, rows), f32), shape((2, half, rows), f32)
    first_t, second_t, third_t = wide(first_t), wide(weight_second.T), wide(third_own.T)
    upper, lower, cos_one, cos_two, window, spec = pl.pallas_call(
        front_kernel,
        out_shape=(joint, joint, act, act, window_shape, spec_shape),
        grid=(STEPS,),
        in_specs=[moving(feats)]
        + [still(a) for a in (first_t, second_t, third_t, params, stage, in_hi, in_lo, turns)],
        out_specs=[moving(2 * hidden + feats)] * 2
        + [moving(hidden)] * 2
        + [still(window_shape), still(spec_shape)],
        scratch_shapes=[pltpu.VMEM((half, rows), f32)],
        name="front",
    )(features, first_t, second_t, third_t, params, stage, in_hi, in_lo, turns)

    operands = (packed, embed_own, params, window, stage, stage_back, in_hi, in_lo, turns)
    second_own = wide(weight_second)
    third_wide = wide(jnp.pad(third_own, ((0, 0), (0, lanes))))
    hidden_shape = shape((groups, hidden // groups, 128), f32)
    third_shape = shape((lanes, hidden), f32)
    results = (hidden_shape, third_shape) + (window_shape,) * 3
    hidden_part, third_part, embedded_all, inner_sum, grad_keyed = pl.pallas_call(
        filter_kernel,
        out_shape=results,
        grid=(STEPS,),
        in_specs=[still(a) for a in operands]
        + [moving(2 * hidden + feats)] * 2
        + [moving(hidden)] * 2
        + [still(second_own), still(third_wide), still(spec)],
        out_specs=[still(a) for a in results],
        scratch_shapes=[
            pltpu.VMEM((half, rows), f32),
            pltpu.VMEM((2 * lanes + 2 * hidden, 2 * hidden + feats), f32),
        ],
        name="filter",
    )(*operands, upper, lower, cos_one, cos_two, second_own, third_wide, spec)

    hidden_part = lax.all_to_all(hidden_part, "chan", 0, 0, tiled=True)
    sent = pl.pallas_call(
        send_kernel,
        out_shape=shape((parts, 5 * lanes + hidden // groups, 128), f32),
        in_specs=[whole] * 6,
        out_specs=whole,
        scratch_shapes=[pltpu.VMEM((parts, 2 * lanes, rows), bf16)],
        name="send",
    )(packed, params, embedded_all, inner_sum, grad_keyed, third_part)
    hidden_sum = jnp.sum(hidden_part, axis=0)
    spread = jnp.broadcast_to(hidden_sum[None], (parts,) + hidden_sum.shape)
    sent = lax.dynamic_update_slice(sent, spread, (0, 5 * lanes, 0))

    vocab_ids = jnp.arange(vocab_size, dtype=jnp.int32)
    before = lax.dynamic_index_in_dim(packed, jnp.maximum(seq_index - 1, 0), 0, keepdims=False)
    before = before[4 * lanes + 1, 126:].astype(jnp.int32)
    before = jnp.where(seq_index > 0, before, -1)
    window_ids = jnp.concatenate([before, tokens])
    lookup = (window_ids[:, None] == vocab_ids[None, :]).astype(bf16)
    embedded = jnp.dot(lookup, embed_table, preferred_element_type=f32)
    value_rows = (
        short_conv[0] * embedded[2:]
        + short_conv[1] * embedded[1:-1]
        + short_conv[2] * embedded[:-2]
    )
    got = lax.all_to_all(sent, "seq", 0, 0, tiled=True)

    hidden_sum = jnp.sum(got[:, 5 * lanes :], axis=0)
    spread = jnp.broadcast_to(hidden_sum[None], (groups,) + hidden_sum.shape)
    total = lax.all_to_all(spread, "chan", 0, 0, tiled=True).reshape(hidden, 128)
    grad_second = total[:, :hidden].T
    grad_first = total[:, hidden : hidden + weight_first.shape[0]].T

    rows_shape = shape((rows, width), bf16)
    own_vocab = vocab_size // parts
    operator_out, grad_query, grad_key, grad_embed, grad_short, grad_skip, grad_third = pl.pallas_call(
        finish_kernel,
        out_shape=(
            rows_shape,
            rows_shape,
            rows_shape,
            shape((own_vocab, width), f32),
            shape((3, width), f32),
            shape((1, width), f32),
            shape((hidden, width), f32),
        ),
        in_specs=[whole] * 4,
        out_specs=[whole] * 7,
        name="finish",
    )(got, query_branch, cotangent, value_rows)
    return (
        operator_out,
        grad_query,
        grad_key,
        grad_embed,
        grad_short,
        grad_skip.reshape(width),
        grad_first,
        grad_second,
        grad_third,
    )


def solution(mesh):
    in_specs = (
        P("seq"),
        P(None, "chan"),
        P(None, "chan"),
        P("seq", "chan"),
        P("seq", "chan"),
        P("chan"),
        P(),
        P(),
        P(None, "chan"),
        P("chan"),
        P("seq", "chan"),
    )
    out_specs = (
        P("seq", "chan"),
        P("seq", "chan"),
        P("seq", "chan"),
        P("seq", "chan"),
        P(None, "chan"),
        P("chan"),
        P(),
        P(),
        P(None, "chan"),
    )
    return jax.shard_map(
        per_device, mesh=mesh, in_specs=in_specs, out_specs=out_specs, check_vma=False
    )
```

```python
import math

import jax
import jax.numpy as jnp
import numpy as np
from jax import lax
from jax.experimental import pallas as pl
from jax.experimental.pallas import tpu as pltpu
from jax.sharding import PartitionSpec as P

BANDS = 16
STEPS = 4
VOCAB = 256

two_pi = 2.0 * math.pi
f32 = jnp.float32
bf16 = jnp.bfloat16


def halves(table):
    upper = np.asarray(np.asarray(table, np.float32), bf16)
    lower = np.asarray(np.asarray(table, np.float32) - np.asarray(upper, np.float32), bf16)
    return upper, lower


def transform_tables(parts, rows, lanes):
    length = parts * rows
    freq = 4 * np.arange(parts, dtype=np.int64) + 1
    phase = freq[:, None] * np.arange(parts, dtype=np.int64)[None, :] % (4 * parts)
    angle = two_pi * phase / (4 * parts)
    stage = np.concatenate([np.cos(angle), -np.sin(angle)], axis=0)
    turn = freq[:, None] * np.arange(rows, dtype=np.int64)[None, :] % (4 * length)
    turn = two_pi * turn / (4 * length)
    inner = np.arange(rows, dtype=np.int64)
    inner = two_pi * (inner[:, None] * inner[None, :] % rows) / rows
    inner = np.concatenate([np.cos(inner), np.sin(inner)], axis=1)
    turns = np.stack([np.cos(turn), np.sin(turn)]).astype(np.float32)
    stages = [np.repeat(table, lanes, axis=1).astype(np.float32) for table in (stage, stage.T)]
    return stages, halves(inner), turns


def feature_table(length):
    positions = np.arange(length, dtype=np.int64)
    frequency = 2 ** np.arange(BANDS, dtype=np.int64) + 1
    phases = frequency[:, None] * positions[None, :] % length
    angles = two_pi * phases / length
    table = np.concatenate([positions[None, :] / length, np.cos(angles), np.sin(angles)], axis=0)
    spare = -table.shape[0] % 16
    return np.asarray(np.pad(table, ((0, spare), (0, 0))), np.float32)


def split(block):
    upper = block.astype(bf16)
    return upper, (block - upper.astype(f32)).astype(bf16)


def dot(left, right):
    return jnp.dot(left, right, preferred_element_type=f32)


def dot_last(left, right):
    return lax.dot_general(left, right, (((1,), (1,)), ((), ())), preferred_element_type=f32)


def product(left, right, by=dot):
    return by(left[0], right[0]) + (by(left[1], right[0]) + by(left[0], right[1]))


def product_last(left, right):
    return product(left, right, dot_last)


def deep(pair):
    return jnp.concatenate([pair[0], pair[0], pair[1]], axis=0)


def wide(matrix):
    upper = lax.reduce_precision(matrix, 8, 7)
    return jnp.concatenate([upper, matrix - upper, upper], axis=1).astype(bf16)


def sine_cosine(angle):
    turns = jnp.floor(angle * (2.0 / math.pi) + 0.5)
    rest = angle - turns * 1.5703125
    rest = rest - turns * 4.837512969970703125e-4
    rest = rest - turns * 7.54978995489188216e-8
    square = rest * rest
    sine = ((-1.9515295891e-4 * square + 8.3321608736e-3) * square - 1.6666654611e-1) * square
    sine = sine * rest + rest
    cosine = (2.443315711809948e-5 * square - 1.388731625493765e-3) * square
    cosine = (cosine + 4.166664568298827e-2) * square * square - 0.5 * square + 1.0
    quarter = turns.astype(jnp.int32)
    odd = (quarter & 1) == 1
    sine, cosine = jnp.where(odd, cosine, sine), jnp.where(odd, sine, cosine)
    sine = jnp.where((quarter & 2) == 2, -sine, sine)
    cosine = jnp.where(((quarter + 1) & 2) == 2, -cosine, cosine)
    return sine, cosine


def spread_stage(table_ref, lanes):
    table = table_ref[...]
    count, width = table.shape
    wide = jnp.broadcast_to(table[:, None, :], (count, lanes, width)).reshape(count * lanes, width)
    row = lax.broadcasted_iota(jnp.int32, wide.shape, 0) & (lanes - 1)
    column = lax.broadcasted_iota(jnp.int32, wide.shape, 1) & (lanes - 1)
    return split(jnp.where(row == column, wide, 0.0))


def spread_turns(turn_ref, lanes):
    def one(table):
        parts, rows = table.shape
        wide = jnp.broadcast_to(table[:, None, :], (parts, lanes, rows))
        return wide.reshape(parts * lanes, rows)

    return one(turn_ref[0]), one(turn_ref[1])


def forward(block, first, inner, turns):
    half, rows = block.shape
    stage = product(first, split(block))
    real, imag = stage[:half], stage[half:]
    turned_real = real * turns[0] + imag * turns[1]
    turned_imag = imag * turns[0] - real * turns[1]
    along = product(split(turned_real), inner)
    across = product(split(turned_imag), inner)
    return along[:, :rows] + across[:, rows:], across[:, :rows] - along[:, rows:]


def inverse(spectrum, first_back, inner, turns, length):
    half, rows = spectrum[0].shape
    along = product(split(spectrum[0]), inner)
    across = product(split(spectrum[1]), inner)
    real = along[:, :rows] - across[:, rows:]
    imag = across[:, :rows] + along[:, rows:]
    turned_real = real * turns[0] - imag * turns[1]
    turned_imag = imag * turns[0] + real * turns[1]
    turned = jnp.concatenate([turned_real, turned_imag], axis=0)
    return product(first_back, split(turned)) * (1.0 / length)


def times(left, right):
    return left[0] * right[0] - left[1] * right[1], left[0] * right[1] + left[1] * right[0]


def against(left, right):
    return left[0] * right[0] + left[1] * right[1], left[0] * right[1] - left[1] * right[0]


def shift_back(block, lanes, steps):
    rolled = pltpu.roll(block, steps, 1)
    before = jnp.concatenate([jnp.zeros_like(rolled[:lanes]), rolled[:-lanes]], axis=0)
    column = lax.broadcasted_iota(jnp.int32, block.shape, 1)
    return jnp.where(column < steps, before, rolled)


def shift_ahead(block, lanes, steps):
    width = block.shape[1]
    rolled = pltpu.roll(block, width - steps, 1)
    after = jnp.concatenate([rolled[lanes:], jnp.zeros_like(rolled[:lanes])], axis=0)
    column = lax.broadcasted_iota(jnp.int32, block.shape, 1)
    return jnp.where(column >= width - steps, after, rolled)


def pack_kernel(key_ref, query_ref, cotangent_ref, token_ref, out_ref):
    parts = out_ref.shape[0]
    rows = key_ref.shape[0]
    lanes = key_ref.shape[1] // parts
    key_cols = key_ref[...].astype(f32).T
    grad_cols = (cotangent_ref[...].astype(f32) * query_ref[...].astype(f32)).T
    place = 0
    for block in (key_cols, grad_cols):
        for start in range(0, rows, 128):
            piece = block[:, start : start + 128].reshape(parts, lanes, 128)
            out_ref[:, place : place + lanes, :] = piece
            place += lanes
    ids = token_ref[...].astype(f32)
    ids = jnp.concatenate([ids, jnp.zeros((lanes - ids.shape[0], 128), f32)], axis=0)
    out_ref[:, place : place + lanes, :] = jnp.broadcast_to(ids[None], (parts, lanes, 128))


def front_kernel(
    feature_ref,
    first_ref,
    second_ref,
    third_ref,
    param_ref,
    stage_ref,
    in_hi,
    in_lo,
    turn_ref,
    upper_ref,
    lower_ref,
    cos_one_ref,
    cos_two_ref,
    window_ref,
    spec_ref,
    filter_ref,
):
    step = pl.program_id(0)
    lanes = third_ref.shape[0]
    half, rows = window_ref.shape
    length = half // lanes * rows
    block = feature_ref.shape[1]
    feature = split(feature_ref[...])
    act_one, cos_one = sine_cosine(dot(first_ref[...], deep(feature)))
    cos_one_ref[...] = cos_one
    act_one = split(act_one)
    act_two, cos_two = sine_cosine(dot(second_ref[...], deep(act_one)))
    cos_two_ref[...] = cos_two
    act_two = split(act_two)
    shaped = dot(third_ref[...], deep(act_two))
    for ref, half_of in ((upper_ref, 0), (lower_ref, 1)):
        both = (act_two[half_of], act_one[half_of], feature[half_of])
        ref[...] = jnp.concatenate(both, axis=0)
    count = block // rows
    for part in range(count):
        place = pl.multiple_of((step * count + part) * lanes, lanes)
        filter_ref[pl.ds(place, lanes), :] = shaped[:, part * rows : (part + 1) * rows]

    @pl.when(step == STEPS - 1)
    def _():
        row = lax.broadcasted_iota(jnp.int32, (half, rows), 0)
        column = lax.broadcasted_iota(jnp.int32, (half, rows), 1)
        position = (row // lanes * rows + column).astype(f32)
        window = param_ref[:, 1:2] * jnp.exp(-param_ref[:, 0:1] * position)
        window_ref[...] = window
        first = spread_stage(stage_ref, lanes)
        inner = (in_hi[...], in_lo[...])
        turns = spread_turns(turn_ref, lanes)
        real, imag = forward(filter_ref[...] * window, first, inner, turns)
        spec_ref[0] = real
        spec_ref[1] = imag


def received(packed_ref, place, lanes):
    parts = packed_ref.shape[0]
    pair = [
        packed_ref[:, at : at + lanes, :].reshape(parts * lanes, 128)
        for at in (place, place + lanes)
    ]
    return jnp.concatenate(pair, axis=1)


def matches(packed_ref, part, lanes, vocab):
    ids = packed_ref[part, 4 * lanes : 4 * lanes + 2, :]
    ids = jnp.concatenate([ids[0:1], ids[1:2]], axis=1)
    ids = jnp.broadcast_to(ids, (16, ids.shape[1])).astype(bf16)
    names = lax.broadcasted_iota(jnp.int32, (vocab, ids.shape[1]), 0).astype(f32).astype(bf16)
    names = names.reshape(vocab // 16, 16, ids.shape[1])
    one, zero = jnp.ones((), bf16), jnp.zeros((), bf16)
    return jnp.where(names == ids[None], one, zero).reshape(vocab, ids.shape[1])


def lagged_values(embedded, param_ref, lanes):
    lagged = [embedded, shift_back(embedded, lanes, 1), shift_back(embedded, lanes, 2)]
    gains = [param_ref[:, 3 + lag : 4 + lag] for lag in range(3)]
    return lagged, gains, gains[0] * lagged[0] + gains[1] * lagged[1] + gains[2] * lagged[2]


def filter_kernel(
    packed_ref,
    embed_ref,
    param_ref,
    window_ref,
    stage_ref,
    back_ref,
    in_hi,
    in_lo,
    turn_ref,
    upper_ref,
    lower_ref,
    cos_one_ref,
    cos_two_ref,
    second_ref,
    third_ref,
    spec_ref,
    hidden_ref,
    third_part_ref,
    embedded_ref,
    inner_ref,
    grad_ref,
    shaped_ref,
    acc_ref,
):
    step = pl.program_id(0)
    parts = packed_ref.shape[0]
    half, rows = window_ref.shape
    lanes = half // parts
    length = parts * rows
    vocab = embed_ref.shape[1]
    hidden = second_ref.shape[0]

    @pl.when(step == 0)
    def _():
        acc_ref[...] = jnp.zeros_like(acc_ref)
        table = embed_ref[...]

        def look_up(part, carry):
            place = pl.multiple_of(part * lanes, lanes)
            found = dot(table, matches(packed_ref, part, lanes, vocab))
            embedded_ref[pl.ds(place, lanes), :] = found
            return carry

        lax.fori_loop(0, parts, look_up, 0, unroll=8)
        key_all = received(packed_ref, 0, lanes)
        grad_z = received(packed_ref, 2 * lanes, lanes)
        _, _, value = lagged_values(embedded_ref[...], param_ref, lanes)
        keyed = key_all * value
        first = spread_stage(stage_ref, lanes)
        first_back = spread_stage(back_ref, lanes)
        inner = (in_hi[...], in_lo[...])
        turns = spread_turns(turn_ref, lanes)
        keyed_spec = forward(keyed, first, inner, turns)
        grad_spec = forward(grad_z, first, inner, turns)
        back = lambda spectrum: inverse(spectrum, first_back, inner, turns, length)
        shaped_ref[...] = back(against(keyed_spec, grad_spec)) * window_ref[...]
        filter_spec = (spec_ref[0], spec_ref[1])
        skip_gain = param_ref[:, 2:3]
        inner_ref[...] = back(times(keyed_spec, filter_spec)) + skip_gain * keyed
        grad_ref[...] = back(against(filter_spec, grad_spec)) + skip_gain * grad_z

    block = upper_ref.shape[1]
    count = block // rows
    pieces = []
    for part in range(count):
        place = pl.multiple_of((step * count + part) * lanes, lanes)
        pieces.append(shaped_ref[pl.ds(place, lanes), :])
    grad_shaped = jnp.concatenate(pieces, axis=1)
    grad_shaped = split(jnp.concatenate([grad_shaped, jnp.zeros_like(grad_shaped)], axis=0))
    grad_pre_two = split(dot(third_ref[...], deep(grad_shaped)) * cos_two_ref[...])
    grad_pre_one = split(dot(second_ref[...], deep(grad_pre_two)) * cos_one_ref[...])
    left = [
        jnp.concatenate([grad_shaped[i], grad_pre_two[i], grad_pre_one[i]], axis=0) for i in range(2)
    ]
    count = left[0].shape[0]
    both = dot_last(jnp.concatenate(left, axis=0), upper_ref[...])
    acc_ref[...] += both[:count] + both[count:] + dot_last(left[0], lower_ref[...])

    @pl.when(step == STEPS - 1)
    def _():
        inv_root = 1.0 / math.sqrt(length)
        two, one = 2 * lanes, 2 * lanes + hidden
        third_part_ref[...] = acc_ref[0:lanes, 0:hidden]
        second_part = acc_ref[two:one, hidden : 2 * hidden]
        first_part = acc_ref[one:, 2 * hidden :]
        spare = jnp.zeros((hidden, hidden - first_part.shape[1]), f32)
        joined = jnp.concatenate([second_part, first_part, spare], axis=1) * inv_root
        hidden_ref[...] = joined.reshape(hidden_ref.shape)


def send_kernel(
    packed_ref, param_ref, embedded_ref, inner_ref, grad_ref, third_ref, out_ref, pieces_ref
):
    parts = packed_ref.shape[0]
    half, rows = embedded_ref.shape
    lanes = half // parts
    hidden = third_ref.shape[1]
    key_all = received(packed_ref, 0, lanes)
    grad_z = received(packed_ref, 2 * lanes, lanes)
    lagged, gains, value = lagged_values(embedded_ref[...], param_ref, lanes)
    grad_keyed = grad_ref[...]
    place = 0
    for block in (inner_ref[...], grad_keyed):
        for start in range(0, rows, 128):
            piece = block[:, start : start + 128].reshape(parts, lanes, 128)
            out_ref[:, place : place + lanes, :] = piece
            place += lanes
    grad_value = grad_keyed * key_all

    def per_channel(block):
        return jnp.sum(jnp.sum(block.reshape(parts, lanes, rows), axis=0), axis=1, keepdims=True)

    tails = [per_channel(grad_value * lagged[lag]) for lag in range(3)]
    tails.append(per_channel(grad_z * (key_all * value)))
    scattered = gains[0] * grad_value
    for lag in (1, 2):
        scattered = scattered + gains[lag] * shift_ahead(grad_value, lanes, lag)
    upper, lower = split(scattered)
    both = (upper.reshape(parts, lanes, rows), lower.reshape(parts, lanes, rows))
    pieces_ref[...] = jnp.concatenate(both, axis=1)

    def collect(part, total):
        return total + dot_last(pieces_ref[part], matches(packed_ref, part, lanes, VOCAB))

    total = lax.fori_loop(0, parts, collect, jnp.zeros((2 * lanes, VOCAB), f32), unroll=8)
    embed_part = total[:lanes] + total[lanes:]
    share = VOCAB // parts
    low, high = 4 * lanes, 5 * lanes
    out_ref[:, low:high, :] = jnp.zeros((parts, lanes, 128), f32)
    for part in range(parts):
        own = embed_part[:, part * share : (part + 1) * share]
        out_ref[part, low:high, 0:share] = own
    third_part = jnp.broadcast_to(third_ref[...][None], (parts, lanes, hidden))
    out_ref[:, low:high, 128 - hidden : 128] = third_part
    for at, tail in enumerate(tails):
        out_ref[:, low:high, 16 + at : 17 + at] = jnp.broadcast_to(tail[None], (parts, lanes, 1))


def finish_kernel(
    packed_ref,
    query_ref,
    cotangent_ref,
    value_ref,
    out_ref,
    grad_query_ref,
    grad_key_ref,
    embed_ref,
    short_ref,
    skip_ref,
    third_ref,
):
    parts = packed_ref.shape[0]
    width = query_ref.shape[1]
    rows = query_ref.shape[0]
    lanes = width // parts
    inv_root = 1.0 / math.sqrt(parts * rows)

    def crossed(place):
        tile = lambda at: packed_ref[:, at : at + lanes, :].reshape(width, 128)
        return jnp.concatenate([tile(place).T, tile(place + lanes).T], axis=0)

    inner_sum = crossed(0)
    out_ref[...] = (query_ref[...].astype(f32) * inner_sum).astype(bf16)
    grad_query_ref[...] = (cotangent_ref[...].astype(f32) * inner_sum).astype(bf16)
    grad_key_ref[...] = (crossed(2 * lanes) * value_ref[...]).astype(bf16)
    small = packed_ref[:, 4 * lanes : 5 * lanes, :].reshape(width, 128).T * inv_root
    embed_ref[...] = small[0 : embed_ref.shape[0]]
    short_ref[...] = small[16:19]
    skip_ref[...] = small[19:20]
    third_ref[...] = small[128 - third_ref.shape[0] :]


def per_device(
    tokens,
    embed_table,
    short_conv,
    query_branch,
    key_branch,
    decay_rate,
    weight_first,
    weight_second,
    weight_third,
    skip_gain,
    cotangent,
):
    parts = lax.axis_size("seq")
    groups = lax.axis_size("chan")
    seq_index = lax.axis_index("seq")
    rows, width = query_branch.shape
    lanes = width // parts
    half = parts * lanes
    length = rows * parts
    vocab_size = embed_table.shape[0]
    hidden = weight_first.shape[1]
    own = seq_index * lanes
    shape = jax.ShapeDtypeStruct
    chunk = (parts, 5 * lanes, 128)
    whole = pl.BlockSpec(memory_space=pltpu.VMEM)

    packed = pl.pallas_call(
        pack_kernel,
        out_shape=shape(chunk, f32),
        in_specs=[whole] * 4,
        out_specs=whole,
        name="pack",
    )(key_branch, query_branch, cotangent, tokens.reshape(rows // 128, 128))
    packed = lax.all_to_all(packed, "seq", 0, 0, tiled=True)

    embed_own = lax.dynamic_slice_in_dim(embed_table, own, lanes, axis=1).T
    short_own = lax.dynamic_slice_in_dim(short_conv, own, lanes, axis=1)
    decay_own = lax.dynamic_slice_in_dim(decay_rate, own, lanes, axis=0)
    skip_own = lax.dynamic_slice_in_dim(skip_gain, own, lanes, axis=0)
    third_own = lax.dynamic_slice_in_dim(weight_third, own, lanes, axis=1)
    scaling = jnp.sqrt(jnp.expm1(-2.0 * decay_own) / jnp.expm1(-2.0 * length * decay_own))
    params = [decay_own, scaling, skip_own, short_own[0], short_own[1], short_own[2]]
    params = jnp.tile(jnp.stack(params + [skip_own, skip_own], axis=1), (parts, 1))

    (stage, stage_back), (in_hi, in_lo), turns = transform_tables(parts, rows, lanes)
    features = jnp.asarray(feature_table(length))
    feats = features.shape[0]
    first_t = jnp.pad(weight_first.T, ((0, 0), (0, feats - weight_first.shape[0])))
    block = length // STEPS
    still = lambda array: pl.BlockSpec(array.shape, lambda i: (0,) * array.ndim)
    moving = lambda count: pl.BlockSpec((count, block), lambda i: (0, i))

    act, joint = shape((hidden, length), f32), shape((2 * hidden + feats, length), bf16)
    window_shape, spec_shape = shape((half, rows), f32), shape((2, half, rows), f32)
    first_t, second_t, third_t = wide(first_t), wide(weight_second.T), wide(third_own.T)
    upper, lower, cos_one, cos_two, window, spec = pl.pallas_call(
        front_kernel,
        out_shape=(joint, joint, act, act, window_shape, spec_shape),
        grid=(STEPS,),
        in_specs=[moving(feats)]
        + [still(a) for a in (first_t, second_t, third_t, params, stage, in_hi, in_lo, turns)],
        out_specs=[moving(2 * hidden + feats)] * 2
        + [moving(hidden)] * 2
        + [still(window_shape), still(spec_shape)],
        scratch_shapes=[pltpu.VMEM((half, rows), f32)],
        name="front",
    )(features, first_t, second_t, third_t, params, stage, in_hi, in_lo, turns)

    operands = (packed, embed_own, params, window, stage, stage_back, in_hi, in_lo, turns)
    second_own = wide(weight_second)
    third_wide = wide(jnp.pad(third_own, ((0, 0), (0, lanes))))
    hidden_shape = shape((groups, hidden // groups, 128), f32)
    third_shape = shape((lanes, hidden), f32)
    results = (hidden_shape, third_shape) + (window_shape,) * 3
    hidden_part, third_part, embedded_all, inner_sum, grad_keyed = pl.pallas_call(
        filter_kernel,
        out_shape=results,
        grid=(STEPS,),
        in_specs=[still(a) for a in operands]
        + [moving(2 * hidden + feats)] * 2
        + [moving(hidden)] * 2
        + [still(second_own), still(third_wide), still(spec)],
        out_specs=[still(a) for a in results],
        scratch_shapes=[
            pltpu.VMEM((half, rows), f32),
            pltpu.VMEM((2 * lanes + 2 * hidden, 2 * hidden + feats), f32),
        ],
        name="filter",
    )(*operands, upper, lower, cos_one, cos_two, second_own, third_wide, spec)

    hidden_part = lax.all_to_all(hidden_part, "chan", 0, 0, tiled=True)
    sent = pl.pallas_call(
        send_kernel,
        out_shape=shape((parts, 5 * lanes + hidden // groups, 128), f32),
        in_specs=[whole] * 6,
        out_specs=whole,
        scratch_shapes=[pltpu.VMEM((parts, 2 * lanes, rows), bf16)],
        name="send",
    )(packed, params, embedded_all, inner_sum, grad_keyed, third_part)
    hidden_sum = jnp.sum(hidden_part, axis=0)
    spread = jnp.broadcast_to(hidden_sum[None], (parts,) + hidden_sum.shape)
    sent = lax.dynamic_update_slice(sent, spread, (0, 5 * lanes, 0))

    vocab_ids = jnp.arange(vocab_size, dtype=jnp.int32)
    before = lax.dynamic_index_in_dim(packed, jnp.maximum(seq_index - 1, 0), 0, keepdims=False)
    before = before[4 * lanes + 1, 126:].astype(jnp.int32)
    before = jnp.where(seq_index > 0, before, -1)
    window_ids = jnp.concatenate([before, tokens])
    lookup = (window_ids[:, None] == vocab_ids[None, :]).astype(bf16)
    embedded = jnp.dot(lookup, embed_table, preferred_element_type=f32)
    value_rows = (
        short_conv[0] * embedded[2:]
        + short_conv[1] * embedded[1:-1]
        + short_conv[2] * embedded[:-2]
    )
    got = lax.all_to_all(sent, "seq", 0, 0, tiled=True)

    hidden_sum = jnp.sum(got[:, 5 * lanes :], axis=0)
    spread = jnp.broadcast_to(hidden_sum[None], (groups,) + hidden_sum.shape)
    total = lax.all_to_all(spread, "chan", 0, 0, tiled=True).reshape(hidden, 128)
    grad_second = total[:, :hidden].T
    grad_first = total[:, hidden : hidden + weight_first.shape[0]].T

    rows_shape = shape((rows, width), bf16)
    own_vocab = vocab_size // parts
    operator_out, grad_query, grad_key, grad_embed, grad_short, grad_skip, grad_third = pl.pallas_call(
        finish_kernel,
        out_shape=(
            rows_shape,
            rows_shape,
            rows_shape,
            shape((own_vocab, width), f32),
            shape((3, width), f32),
            shape((1, width), f32),
            shape((hidden, width), f32),
        ),
        in_specs=[whole] * 4,
        out_specs=[whole] * 7,
        name="finish",
    )(got, query_branch, cotangent, value_rows)
    return (
        operator_out,
        grad_query,
        grad_key,
        grad_embed,
        grad_short,
        grad_skip.reshape(width),
        grad_first,
        grad_second,
        grad_third,
    )


def solution(mesh):
    in_specs = (
        P("seq"),
        P(None, "chan"),
        P(None, "chan"),
        P("seq", "chan"),
        P("seq", "chan"),
        P("chan"),
        P(),
        P(),
        P(None, "chan"),
        P("chan"),
        P("seq", "chan"),
    )
    out_specs = (
        P("seq", "chan"),
        P("seq", "chan"),
        P("seq", "chan"),
        P("seq", "chan"),
        P(None, "chan"),
        P("chan"),
        P(),
        P(),
        P(None, "chan"),
    )
    return jax.shard_map(
        per_device, mesh=mesh, in_specs=in_specs, out_specs=out_specs, check_vma=False
    )
```
